256 devices in a mesh: expert: 64 (over y, z, core), fsdp: 4 (over x).
Axes of the slice: x: 4, y: 4, z: 8, core: 2. Of those that a mesh axis runs over, the one named last changes fastest.
Arguments:
- feats: bfloat16 [1024, 128, 1536], P('expert', None, 'fsdp'), may hold values from -6 to 6
- cotan: bfloat16 [1024, 128, 1536], P('expert', None, 'fsdp'), may hold values from -6 to 6
- lang: int32 [1024], P('expert'), may hold values from 0 to 63, as said below
- w_out: bfloat16 [64, 1536, 1536], P('expert', 'fsdp'), may hold values from -0.15625 to 0.15625
- gain: bfloat16 [64, 1536], P('expert', 'fsdp'), may hold values from 0.099609375 to 1.8984375
- kernel: bfloat16 [64, 31, 1536], P('expert', None, 'fsdp'), may hold values from -1 to 1
Outputs:
- feat_grad: bfloat16 [1024, 128, 1536], P('expert', None, 'fsdp')
- w_grad: bfloat16 [64, 1536, 1536], P('expert', 'fsdp')
- gain_grad: float32 [64, 1536], P('expert', 'fsdp')
- kernel_grad: float32 [64, 31, 1536], P('expert', None, 'fsdp')
The draws below stay inside these ranges and needn't reach their ends.
Inputs may be any that keep to these rules, and one draw needn't show every extreme that they name: `lang`: each index of the expert axis holds either none or exactly 1 segments of a language, and each language has exactly 16 segments in all.
All inputs are finite; a program needn't handle non-finite values.
Results may differ from the reference program's by a relative error of at most 0.005.
Values may be sent and summed in bfloat16 or wider, within the bound.
A program may use at most 128 MiB of HBM per device.

```python
import jax
import jax.numpy as jnp
from jax import lax

D = 1536
KERNEL = 31
FRAMES = 128
SEGS = 16
CAP = 1
SEG_COL = 1024
N_EXPERT = 64


def draw_lang(key, part):
    first_key, second_key = jax.random.split(key, 2)
    col_keys = jax.random.randint(first_key, (N_EXPERT,), 0, 1 << 20)
    perms = jnp.argsort(col_keys * N_EXPERT + jnp.arange(N_EXPERT)).astype(jnp.int32)
    seg_keys = jax.random.randint(second_key, (N_EXPERT, SEGS), 0, 1 << 20)
    shuffles = jnp.argsort(seg_keys * SEGS + jnp.arange(SEGS)[None, :], axis=1).astype(jnp.int32)
    group_index = shuffles // CAP
    source = jnp.arange(N_EXPERT, dtype=jnp.int32)[:, None]
    residue = (source * (SEGS // CAP) + group_index) % N_EXPERT
    language = perms[residue.reshape(N_EXPERT * SEGS)]
    return language.astype(jnp.int32)


def levels(key, extent, cuts, least, largest):
    loudness = 1.0
    for dim, shards_of in cuts:
        steps = jax.random.uniform(jax.random.fold_in(jax.random.fold_in(key, 6), dim), (shards_of,), jnp.float32, least / len(cuts), largest / len(cuts))
        loudness = loudness * jnp.repeat(jnp.exp(steps), extent[dim] // shards_of).reshape((-1,) + (1,) * (len(extent) - 1 - dim))
    return loudness


def normal_values(stream_key, shape, scale, reach, cuts=(), held_as=jnp.bfloat16):
    drawn = jax.random.normal(stream_key, shape, jnp.float32) * scale
    if len(cuts) > 0:
        drawn = levels(stream_key, shape, cuts, -0.22, 0.18) * drawn
    return jnp.clip(drawn, min=-reach, max=reach).astype(held_as)


def setup_inputs(seed: int = 0) -> dict:
    seeds = jax.random.split(jax.random.key(seed), 7)
    return {
        "feats": normal_values(seeds[0], (SEG_COL, FRAMES, D), 1.0, 6.0, ((0, 64), (2, 4))),
        "cotan": normal_values(seeds[1], (SEG_COL, FRAMES, D), 1.0, 6.0, ((0, 64), (2, 4))),
        "lang": draw_lang(jax.random.fold_in(seeds[6], 71), 0),
        "w_out": normal_values(seeds[3], (N_EXPERT, D, D), D ** -0.5, 0.15625, ((0, 64), (1, 4))),
        "gain": jnp.clip(1.0 + 0.18 * jax.random.normal(seeds[4], (N_EXPERT, D), jnp.float32), 0.099609375, 1.8984375).astype(jnp.bfloat16),
        "kernel": normal_values(seeds[5], (N_EXPERT, KERNEL, D), KERNEL ** -0.5, 1.0, ((0, 64), (2, 4))),
    }


def front(inputs, norm_gain, conv_taps):
    values = inputs.astype(jnp.float32)
    centre = values - lax.optimization_barrier(jnp.mean(values, axis=-1, keepdims=True))
    inv_std = lax.rsqrt(lax.optimization_barrier(jnp.mean(centre * centre, axis=-1, keepdims=True)) + 1e-05)
    normed = centre * inv_std
    scaled = normed * norm_gain
    tap_count = conv_taps.shape[0]
    half_width = tap_count // 2
    frames = inputs.shape[1]
    padded = jnp.pad(scaled, ((0, 0), (half_width, half_width), (0, 0)))
    conv_out = jnp.zeros_like(scaled)
    for offset in range(tap_count):
        conv_out = conv_out + conv_taps[offset] * padded[:, offset:offset + frames]
    gate_sig = jax.nn.sigmoid(conv_out)
    hidden = (conv_out * gate_sig).astype(jnp.bfloat16)
    return (normed, inv_std, padded, conv_out, gate_sig, hidden)

def back(hid_grad, grads_in, normed, inv_std, padded, conv_out, gate_sig, norm_gain, conv_taps):
    tap_count = conv_taps.shape[0]
    half_width = tap_count // 2
    frames = normed.shape[1]
    conv_grad = hid_grad * gate_sig * (1.0 + conv_out * (1.0 - gate_sig))
    grad_padded = jnp.pad(conv_grad, ((0, 0), (half_width, half_width), (0, 0)))
    scaled_grad = jnp.zeros_like(conv_grad)
    tap_grads = []
    for offset in range(tap_count):
        first_row = 2 * half_width - offset
        scaled_grad = scaled_grad + conv_taps[offset] * grad_padded[:, first_row:first_row + frames]
        tap_grads.append(lax.optimization_barrier(jnp.sum(conv_grad * padded[:, offset:offset + frames], axis=(0, 1))))
    gain_grad = lax.optimization_barrier(jnp.sum(scaled_grad * normed, axis=(0, 1)))
    norm_grad = scaled_grad * norm_gain
    branch = inv_std * (norm_grad - lax.optimization_barrier(jnp.mean(norm_grad, axis=-1, keepdims=True)) - normed * lax.optimization_barrier(jnp.mean(norm_grad * normed, axis=-1, keepdims=True)))
    input_grad = (grads_in.astype(jnp.float32) + branch).astype(jnp.bfloat16)
    return (input_grad, gain_grad, jnp.stack(tap_grads))

def reference(feats, cotan, lang, w_out, gain, kernel):
    orders = jnp.argsort(lang, stable=True).astype(jnp.int32)
    grouped = orders.reshape(N_EXPERT, SEGS)
    grad_scale = float(SEGS * FRAMES) ** (-0.5)

    def per_expert(operands):
        rows_e, weight_e, gain_e, taps_e = operands
        xs_e = feats[rows_e]
        dys_e = cotan[rows_e]
        norm_gain = gain_e.astype(jnp.float32)
        conv_taps = taps_e.astype(jnp.float32)
        normed, inv_std, padded, conv_out, gate_sig, hidden = front(xs_e, norm_gain, conv_taps)
        dy_rows = dys_e.reshape(-1, D)
        hid_grad = jnp.dot(dy_rows, weight_e.T, preferred_element_type=jnp.float32).reshape(normed.shape)
        input_grad, gain_grad, tap_grad = back(hid_grad, dys_e, normed, inv_std, padded, conv_out, gate_sig, norm_gain, conv_taps)
        weight_grad = jnp.dot(hidden.reshape(-1, D).T, dy_rows, preferred_element_type=jnp.float32) * grad_scale
        return (input_grad, weight_grad.astype(jnp.bfloat16), gain_grad * grad_scale, tap_grad * grad_scale)
    grads_sorted, w_grad, gain_grad, kernel_grad = lax.map(per_expert, (grouped, w_out, gain, kernel))
    inverse = jnp.argsort(orders).astype(jnp.int32)
    feat_grad = grads_sorted.reshape(N_EXPERT * SEGS, FRAMES, D)[inverse]
    return (feat_grad, w_grad, gain_grad, kernel_grad)
```

```python
import functools

import jax
import jax.numpy as jnp
from jax import lax
from jax.experimental import pallas as pl
from jax.experimental.pallas import tpu as pltpu
from jax.sharding import PartitionSpec as P

MESH = pl.DeviceIdType.MESH
F32 = jnp.float32
BF16 = jnp.bfloat16
LANES = 128
STEP = 8


def swap_kernel(v_ref, o_ref):
    o_ref[...] = jnp.swapaxes(v_ref[...].astype(F32), 0, 1).astype(BF16)


def to_frames(values):
    segs, frames, width = values.shape
    block = 16
    return pl.pallas_call(
        swap_kernel,
        out_shape=jax.ShapeDtypeStruct((frames, segs, width), BF16),
        grid=(frames // block,),
        in_specs=[pl.BlockSpec((segs, block, width), lambda i: (0, i, 0))],
        out_specs=pl.BlockSpec((block, segs, width), lambda i: (i, 0, 0)),
        cost_estimate=pl.CostEstimate(flops=values.size, bytes_accessed=4 * values.size, transcendentals=0),
        name="to_frames",
    )(values)


def to_segments(values):
    frames, segs, width = values.shape
    block = 16
    return pl.pallas_call(
        swap_kernel,
        out_shape=jax.ShapeDtypeStruct((segs, frames, width), BF16),
        grid=(frames // block,),
        in_specs=[pl.BlockSpec((block, segs, width), lambda i: (i, 0, 0))],
        out_specs=pl.BlockSpec((segs, block, width), lambda i: (0, i, 0)),
        cost_estimate=pl.CostEstimate(flops=values.size, bytes_accessed=4 * values.size, transcendentals=0),
        name="to_segments",
    )(values)


def permute_kernel(dest_ref, v_ref, o_ref):
    total = dest_ref.shape[1]
    rows = o_ref.shape[0] * o_ref.shape[1]
    first = pl.program_id(1) * rows
    out_row = lax.broadcasted_iota(jnp.int32, (rows, total), 0) + first
    pick = jnp.where(out_row == dest_ref[...], 1.0, 0.0).astype(BF16)
    flat = v_ref[...].reshape(total, v_ref.shape[2])
    moved = jnp.dot(pick, flat, preferred_element_type=F32)
    o_ref[...] = moved.astype(BF16).reshape(o_ref.shape)


def permute(dest, values, segs):
    owners, rows, width = values.shape
    part = 16
    return pl.pallas_call(
        permute_kernel,
        out_shape=jax.ShapeDtypeStruct(values.shape, BF16),
        grid=(rows // segs, owners // part),
        in_specs=[
            pl.BlockSpec((1, owners * segs), lambda j, b: (0, 0)),
            pl.BlockSpec((owners, segs, width), lambda j, b: (0, j, 0)),
        ],
        out_specs=pl.BlockSpec((part, segs, width), lambda j, b: (b, j, 0)),
        cost_estimate=pl.CostEstimate(
            flops=2 * owners * segs * values.size, bytes_accessed=4 * values.size, transcendentals=0
        ),
        name="permute_rows",
    )(dest, values)


def exchange_kernel(n, v_ref, o_ref, send_sem, recv_sem):
    me = lax.axis_index("fsdp")
    barrier = pltpu.get_barrier_semaphore()
    for d in range(1, n):
        pl.semaphore_signal(barrier, inc=1, device_id={"fsdp": lax.rem(me + d, n)}, device_id_type=MESH)
    pl.semaphore_wait(barrier, n - 1)
    copies = []
    for d in range(1, n):
        copy = pltpu.make_async_remote_copy(
            src_ref=v_ref,
            dst_ref=o_ref.at[d],
            send_sem=send_sem.at[d],
            recv_sem=recv_sem.at[d],
            device_id={"fsdp": lax.rem(me + d, n)},
            device_id_type=MESH,
        )
        copy.start()
        copies.append(copy)
    o_ref[0] = v_ref[...]
    for copy in copies:
        copy.wait()


def exchange(values, n, cid):
    return pl.pallas_call(
        functools.partial(exchange_kernel, n),
        out_shape=jax.ShapeDtypeStruct((n,) + values.shape, values.dtype),
        in_specs=[pl.BlockSpec(memory_space=pltpu.VMEM)],
        out_specs=pl.BlockSpec(memory_space=pltpu.VMEM),
        scratch_shapes=[pltpu.SemaphoreType.DMA((n,)), pltpu.SemaphoreType.DMA((n,))],
        compiler_params=pltpu.CompilerParams(collective_id=cid, has_side_effects=True),
        name="exchange_sums",
    )(values)


def diagonal(segs):
    lane = lax.broadcasted_iota(jnp.int32, (1, segs, LANES), 2)
    seg = lax.broadcasted_iota(jnp.int32, (1, segs, LANES), 1)
    return lane == seg, lane == seg + LANES // 2


def to_row(first, second, segs):
    low, high = diagonal(segs)
    spread = jnp.where(low, first, 0.0) + jnp.where(high, second, 0.0)
    return jnp.sum(spread, axis=1)


def to_column(row, segs):
    low, _ = diagonal(segs)
    return jnp.sum(jnp.where(low, row[:, None, :], 0.0), axis=2, keepdims=True)


def moments_kernel(x_ref, o_ref):
    width = x_ref.shape[2]
    segs = x_ref.shape[1]
    x = x_ref[...].astype(F32)
    mean = jnp.sum(x, axis=2, keepdims=True) * (1.0 / width)
    centre = x - mean
    square = jnp.sum(centre * centre, axis=2, keepdims=True)
    o_ref[...] = to_row(mean, square, segs)


def moments(x):
    frames, segs, width = x.shape
    block = 16
    return pl.pallas_call(
        moments_kernel,
        out_shape=jax.ShapeDtypeStruct((frames, LANES), F32),
        grid=(frames // block,),
        in_specs=[pl.BlockSpec((block, segs, width), lambda i: (i, 0, 0))],
        out_specs=pl.BlockSpec((block, LANES), lambda i: (i, 0)),
        name="moments",
    )(x)


def mean_and_scale(parts, width):
    n = parts.shape[0]
    rows = [parts[d] for d in range(n)]
    squares = [pltpu.roll(r, LANES // 2, 1) for r in rows]
    mean = sum(rows) * (1.0 / n)
    spread = sum((r - mean) * (r - mean) for r in rows)
    var = (sum(squares) + width * spread) * (1.0 / (n * width))
    return mean, lax.rsqrt(var + 1e-05)


def forward_kernel(width, parts_ref, x_ref, gain_ref, taps_ref, normed_ref, conv_ref, hidden_ref, mean_c, scale_c, padded, tapb):
    frames, segs, _ = x_ref.shape
    taps = taps_ref.shape[0]
    half = taps // 2

    @pl.when(pl.program_id(0) == 0)
    def _():
        mean, scale = mean_and_scale(parts_ref[...], width)
        mean_c[...] = jnp.broadcast_to(to_column(mean, segs), mean_c.shape)
        scale_c[...] = jnp.broadcast_to(to_column(scale, segs), scale_c.shape)

    edge = jnp.zeros((half, segs, LANES), F32)
    padded[:half] = edge
    padded[half + frames :] = jnp.zeros((padded.shape[0] - half - frames, segs, LANES), F32)
    for k in range(taps):
        tapb[k] = jnp.broadcast_to(taps_ref[k : k + 1, :].astype(F32), (8, LANES))
    gain = gain_ref[...].astype(F32)

    def fill(i, carry):
        t = i * STEP
        normed = (x_ref[pl.ds(t, STEP)].astype(F32) - mean_c[pl.ds(t, STEP)]) * scale_c[pl.ds(t, STEP)]
        normed_ref[pl.ds(t, STEP)] = normed
        padded[pl.ds(t + half, STEP)] = normed * gain[None]
        return carry

    lax.fori_loop(0, frames // STEP, fill, 0)

    def convolve(i, carry):
        t = i * STEP
        for h in range(segs // 8):
            acc = [None] * STEP
            for u in range(STEP + taps - 1):
                v = padded[t + u, h * 8 : h * 8 + 8, :]
                for j in range(STEP):
                    k = u - j
                    if 0 <= k < taps:
                        term = tapb[k] * v
                        acc[j] = term if acc[j] is None else acc[j] + term
            for j in range(STEP):
                conv_ref[t + j, h * 8 : h * 8 + 8, :] = acc[j]
        c = conv_ref[pl.ds(t, STEP)]
        hidden_ref[pl.ds(t, STEP)] = (c / (1.0 + jnp.exp(-c))).astype(BF16)
        return carry

    lax.fori_loop(0, frames // STEP, convolve, 0)


def forward(parts, x, gain, taps):
    frames, segs, width = x.shape
    n_taps = taps.shape[0]
    block = pl.BlockSpec((frames, segs, LANES), lambda i: (0, 0, i))
    return pl.pallas_call(
        functools.partial(forward_kernel, width),
        out_shape=(
            jax.ShapeDtypeStruct(x.shape, F32),
            jax.ShapeDtypeStruct(x.shape, F32),
            jax.ShapeDtypeStruct(x.shape, BF16),
        ),
        grid=(width // LANES,),
        in_specs=[
            pl.BlockSpec(parts.shape, lambda i: (0, 0, 0)),
            block,
            pl.BlockSpec((1, LANES), lambda i: (0, i)),
            pl.BlockSpec((n_taps, LANES), lambda i: (0, i)),
        ],
        out_specs=(block, block, block),
        scratch_shapes=[
            pltpu.VMEM((frames, segs, LANES), F32),
            pltpu.VMEM((frames, segs, LANES), F32),
            pltpu.VMEM((frames + 32, segs, LANES), F32),
            pltpu.VMEM((n_taps, 8, LANES), F32),
        ],
        cost_estimate=pl.CostEstimate(flops=80 * x.size, bytes_accessed=12 * x.size, transcendentals=x.size),
        name="forward",
    )(parts, x, gain, taps)


def hid_kernel(order_ref, d0, d1, d2, d3, w_ref, o_ref):
    width = d0.shape[1]
    total = None
    for j, d in enumerate((d0, d1, d2, d3)):
        cols = pl.ds(pl.multiple_of(order_ref[j] * width, LANES), width)
        term = lax.dot_general(
            d[...], w_ref[:, cols], (((1,), (1,)), ((), ())), preferred_element_type=F32
        )
        total = term if total is None else total + term
    o_ref[...] = total


def hid_grads(order, pieces, w):
    rows, width = pieces[0].shape
    block = 256
    return pl.pallas_call(
        hid_kernel,
        out_shape=jax.ShapeDtypeStruct((rows, w.shape[0]), F32),
        grid_spec=pltpu.PrefetchScalarGridSpec(
            num_scalar_prefetch=1,
            grid=(rows // block,),
            in_specs=[pl.BlockSpec((block, width), lambda i, o: (i, 0))] * 4
            + [pl.BlockSpec(w.shape, lambda i, o: (0, 0))],
            out_specs=pl.BlockSpec((block, w.shape[0]), lambda i, o: (i, 0)),
        ),
        cost_estimate=pl.CostEstimate(flops=2 * rows * w.size, bytes_accessed=8 * rows * width, transcendentals=0),
        name="hid_grads",
    )(order, *pieces, w)


def backward_kernel(scale, hid_ref, conv_ref, normed_ref, gain_ref, taps_ref, sg_ref, kg_ref, gg_ref, row_ref, gpad, spad, tapb, sum_a, sum_b):
    frames, segs, _ = hid_ref.shape
    taps = taps_ref.shape[0]
    half = taps // 2
    step = pl.program_id(0)
    tail = gpad.shape[0] - half - frames
    for pad in (gpad, spad):
        pad[:half] = jnp.zeros((half, segs, LANES), F32)
        pad[half + frames :] = jnp.zeros((tail, segs, LANES), F32)
    for k in range(taps):
        tapb[k] = jnp.broadcast_to(taps_ref[k : k + 1, :].astype(F32), (8, LANES))
    gain = gain_ref[...].astype(F32)

    @pl.when(step == 0)
    def _():
        sum_a[...] = jnp.zeros_like(sum_a)
        sum_b[...] = jnp.zeros_like(sum_b)

    def fill(i, carry):
        t = i * STEP
        c = conv_ref[pl.ds(t, STEP)]
        s = 1.0 / (1.0 + jnp.exp(-c))
        gpad[pl.ds(t + half, STEP)] = hid_ref[pl.ds(t, STEP)] * s * (1.0 + c * (1.0 - s))
        spad[pl.ds(t + half, STEP)] = normed_ref[pl.ds(t, STEP)] * gain[None]
        return carry

    lax.fori_loop(0, frames // STEP, fill, 0)

    def transposed(i, gain_sum):
        t = i * STEP
        for h in range(segs // 8):
            rows = slice(h * 8, h * 8 + 8)
            acc = [None] * STEP
            for u in range(STEP + taps - 1):
                v = gpad[t + u, rows, :]
                for j in range(STEP):
                    k = taps - 1 - (u - j)
                    if 0 <= k < taps:
                        term = tapb[k] * v
                        acc[j] = term if acc[j] is None else acc[j] + term
            for j in range(STEP):
                sg_ref[t + j, rows, :] = acc[j]
                normed = normed_ref[t + j, rows, :]
                cross = acc[j] * normed
                gain_sum = gain_sum + cross
                sum_a[t + j, rows, :] += acc[j] * gain
                sum_b[t + j, rows, :] += cross * gain
        return gain_sum

    gain_sum = lax.fori_loop(0, frames // STEP, transposed, jnp.zeros((8, LANES), F32))
    gg_ref[...] = jnp.sum(gain_sum, axis=0, keepdims=True) * scale

    def tap_sums(i, acc):
        t = i * STEP
        acc = list(acc)
        for h in range(segs // 8):
            rows = slice(h * 8, h * 8 + 8)
            g = [gpad[t + half + j, rows, :] for j in range(STEP)]
            for u in range(STEP + taps - 1):
                v = spad[t + u, rows, :]
                for j in range(STEP):
                    k = u - j
                    if 0 <= k < taps:
                        acc[k] = acc[k] + g[j] * v
        return tuple(acc)

    sums = lax.fori_loop(0, frames // STEP, tap_sums, tuple(jnp.zeros((8, LANES), F32) for _ in range(taps)))
    for k in range(taps):
        kg_ref[k : k + 1, :] = jnp.sum(sums[k], axis=0, keepdims=True) * scale

    @pl.when(step == pl.num_programs(0) - 1)
    def _():
        row_ref[...] = to_row(
            jnp.sum(sum_a[...], axis=2, keepdims=True), jnp.sum(sum_b[...], axis=2, keepdims=True), segs
        )


def backward(hid, conv, normed, gain, taps, scale):
    frames, segs, width = hid.shape
    n_taps = taps.shape[0]
    block = pl.BlockSpec((frames, segs, LANES), lambda i: (0, 0, i))
    row = pl.BlockSpec((1, LANES), lambda i: (0, i))
    tap = pl.BlockSpec((n_taps, LANES), lambda i: (0, i))
    return pl.pallas_call(
        functools.partial(backward_kernel, scale),
        out_shape=(
            jax.ShapeDtypeStruct(hid.shape, F32),
            jax.ShapeDtypeStruct((n_taps, width), F32),
            jax.ShapeDtypeStruct((1, width), F32),
            jax.ShapeDtypeStruct((frames, LANES), F32),
        ),
        grid=(width // LANES,),
        in_specs=[block, block, block, row, tap],
        out_specs=(block, tap, row, pl.BlockSpec((frames, LANES), lambda i: (0, 0))),
        scratch_shapes=[
            pltpu.VMEM((frames + 32, segs, LANES), F32),
            pltpu.VMEM((frames + 32, segs, LANES), F32),
            pltpu.VMEM((n_taps, 8, LANES), F32),
            pltpu.VMEM((frames, segs, LANES), F32),
            pltpu.VMEM((frames, segs, LANES), F32),
        ],
        cost_estimate=pl.CostEstimate(flops=160 * hid.size, bytes_accessed=16 * hid.size, transcendentals=hid.size),
        name="backward",
    )(hid, conv, normed, gain, taps)


def finish_kernel(width, parts_ref, sums_ref, sg_ref, normed_ref, dy_ref, gain_ref, o_ref):
    segs = sg_ref.shape[1]
    n = parts_ref.shape[0]
    _, scale = mean_and_scale(parts_ref[...], width)
    total = sum(sums_ref[d] for d in range(n)) * (1.0 / (n * width))
    scale = to_column(scale, segs)
    plain = to_column(total, segs)
    cross = to_column(pltpu.roll(total, LANES // 2, 1), segs)
    branch = scale * (sg_ref[...] * gain_ref[...].astype(F32)[None] - plain - normed_ref[...] * cross)
    o_ref[...] = (dy_ref[...].astype(F32) + branch).astype(BF16)


def finish(parts, sums, sg, normed, dy, gain):
    frames, segs, width = sg.shape
    n = parts.shape[0]
    block = 16
    rows = pl.BlockSpec((n, block, LANES), lambda i: (0, i, 0))
    spec = pl.BlockSpec((block, segs, width), lambda i: (i, 0, 0))
    return pl.pallas_call(
        functools.partial(finish_kernel, width),
        out_shape=jax.ShapeDtypeStruct(sg.shape, BF16),
        grid=(frames // block,),
        in_specs=[rows, rows, spec, spec, spec, pl.BlockSpec((1, width), lambda i: (0, 0))],
        out_specs=spec,
        name="finish",
    )(parts, sums, sg, normed, dy, gain)


def per_device(feats, cotan, lang, w_out, gain, kernel):
    segs, frames, width = feats.shape
    owners = lax.axis_size("expert")
    shards = lax.axis_size("fsdp")
    per = frames // owners
    me = lax.axis_index("fsdp")
    wire = (owners, per * segs, width)
    grad_scale = float(segs * frames) ** (-0.5)

    def all_to_all(v):
        return lax.all_to_all(v, "expert", split_axis=0, concat_axis=0, tiled=True)

    dy_split = all_to_all(to_frames(cotan).reshape(wire))
    langs = all_to_all(jnp.broadcast_to(lang[None, :], (owners, segs))).reshape(-1)
    x_split = all_to_all(to_frames(feats).reshape(wire))

    count = owners * segs
    index = jnp.arange(count, dtype=jnp.int32)
    earlier = (langs[:, None] == langs[None, :]) & (index[:, None] < index[None, :])
    dest = langs * segs + jnp.sum(earlier.astype(jnp.int32), axis=0)
    source = jnp.sum(jnp.where(dest[:, None] == index[None, :], index[:, None], 0), axis=0)
    dest, source = dest[None, :], source[None, :]

    dy = all_to_all(permute(dest, dy_split, segs))
    x = all_to_all(permute(dest, x_split, segs)).reshape(frames, segs, width)

    up = [(i, (i + 1) % shards) for i in range(shards)]
    down = [(i, (i - 1) % shards) for i in range(shards)]
    rows = dy.reshape(frames * segs, width)
    before = lax.ppermute(rows, "fsdp", up)
    after = lax.ppermute(rows, "fsdp", down)
    half = frames * segs // 2
    across = jnp.concatenate(
        [lax.ppermute(before[:half], "fsdp", up), lax.ppermute(after[half:], "fsdp", down)]
    )
    order = jnp.stack([me, (me + 3) % 4, (me + 1) % 4, (me + 2) % 4]).astype(jnp.int32)

    taps = kernel[0]
    parts = exchange(moments(x), shards, 1)
    normed, conv, hidden = forward(parts, x, gain, taps)
    pieces = (rows, before, after, across)
    hid = hid_grads(order, pieces, w_out[0]).reshape(frames, segs, width)
    scaled_grad, tap_grad, gain_grad, sums = backward(hid, conv, normed, gain, taps, grad_scale)
    sums = exchange(sums, shards, 2)
    grads = finish(parts, sums, scaled_grad, normed, dy.reshape(frames, segs, width), gain)
    back = all_to_all(grads.reshape(wire))
    home = all_to_all(permute(source, back, segs))
    feat_grad = to_segments(home.reshape(frames, segs, width))

    full = jnp.concatenate(pieces, axis=1)
    w_rel = lax.dot_general(
        hidden.reshape(-1, width), full, (((0,), (0,)), ((), ())), preferred_element_type=F32
    )
    w_rel = (w_rel * grad_scale).astype(BF16)
    w_grad = jnp.zeros_like(w_rel)
    for j in range(4):
        w_grad = lax.dynamic_update_slice(w_grad, w_rel[:, j * width : (j + 1) * width], (0, order[j] * width))
    return feat_grad, w_grad[None], gain_grad, tap_grad[None]


def solution(mesh):
    in_specs = (
        P("expert", None, "fsdp"),
        P("expert", None, "fsdp"),
        P("expert"),
        P("expert", "fsdp", None),
        P("expert", "fsdp"),
        P("expert", None, "fsdp"),
    )
    out_specs = (
        P("expert", None, "fsdp"),
        P("expert", "fsdp", None),
        P("expert", "fsdp"),
        P("expert", None, "fsdp"),
    )
    return jax.shard_map(
        per_device, mesh=mesh, in_specs=in_specs, out_specs=out_specs, check_vma=False
    )
```

```python
import functools

import jax
import jax.numpy as jnp
from jax import lax
from jax.experimental import pallas as pl
from jax.experimental.pallas import tpu as pltpu
from jax.sharding import PartitionSpec as P

MESH = pl.DeviceIdType.MESH
F32 = jnp.float32
BF16 = jnp.bfloat16
LANES = 128
STEP = 8
FB = 16


def diagonal(segs):
    lane = lax.broadcasted_iota(jnp.int32, (1, segs, LANES), 2)
    seg = lax.broadcasted_iota(jnp.int32, (1, segs, LANES), 1)
    return lane == seg, lane == seg + LANES // 2


def to_row(first, second, segs):
    low, high = diagonal(segs)
    spread = jnp.where(low, first, 0.0) + jnp.where(high, second, 0.0)
    return jnp.sum(spread, axis=1)


def to_column(row, segs):
    low, _ = diagonal(segs)
    return jnp.sum(jnp.where(low, row[:, None, :], 0.0), axis=2, keepdims=True)


def mean_and_scale(rows, width):
    n = len(rows)
    squares = [pltpu.roll(r, LANES // 2, 1) for r in rows]
    mean = sum(rows) * (1.0 / n)
    spread = sum((r - mean) * (r - mean) for r in rows)
    var = (sum(squares) + width * spread) * (1.0 / (n * width))
    return mean, lax.rsqrt(var + 1e-05)


def module_kernel(
    owners, shards, grad_scale,
    lang_ref, x_ref, dy_ref, w_ref, gain_ref, taps_ref,
    feat_ref, wgrad_ref, ggrad_ref, kgrad_ref,
    langs, s0, s1, r0, r1, dy_own, x_own, ring, pick, pick_t,
    normed, conv, hidden, hid, gpad, spad, tapb, kacc, sum_a, sum_b, scale_c, mom, parts, sums,
    send, recv, ring_send, ring_recv, ex_send, ex_recv,
):
    segs, frames, width = x_ref.shape
    taps = taps_ref.shape[0]
    half = taps // 2
    total = owners * segs
    chunks = width // LANES
    me = lax.axis_index("expert")
    fs = lax.axis_index("fsdp")
    peer_x = [lax.rem(fs + d, shards) for d in range(shards)]

    barrier = pltpu.get_barrier_semaphore()

    def greet(d, carry):
        pl.semaphore_signal(
            barrier, inc=1, device_id={"expert": lax.rem(me + d, owners)}, device_id_type=MESH
        )
        return carry

    lax.fori_loop(1, owners, greet, 0)
    for d in range(1, shards):
        pl.semaphore_signal(barrier, inc=1, device_id={"fsdp": peer_x[d]}, device_id_type=MESH)

    def split_frames(src, dst):
        def block(b, carry):
            rows = src[:, pl.ds(pl.multiple_of(b * FB, FB), FB), :].astype(F32)
            moved = jnp.swapaxes(rows, 0, 1).astype(BF16)
            dst[pl.ds(b * (FB // 2), FB // 2)] = moved.reshape(FB // 2, 2, segs, width)
            return carry

        lax.fori_loop(0, frames // FB, block, 0)

    def scatter(src, dst, i):
        def one(p):
            pltpu.make_async_remote_copy(
                src_ref=src.at[p], dst_ref=dst.at[me], send_sem=send.at[i], recv_sem=recv.at[i],
                device_id={"expert": p}, device_id_type=MESH,
            ).start()

        def both(d, carry):
            one(lax.rem(me + d, owners))
            one(lax.rem(me + owners - d, owners))
            return carry

        lax.fori_loop(1, owners // 2, both, 0)
        one(lax.rem(me + owners // 2, owners))
        pltpu.make_async_copy(src.at[me], dst.at[me], recv.at[i]).start()

    def arrived(src, dst, i):
        pltpu.make_async_copy(src, dst, recv.at[i]).wait()

    def sent(src, dst, i):
        most = pl.ds(0, owners - 1)
        pltpu.make_async_remote_copy(
            src_ref=src.at[most], dst_ref=dst.at[most], send_sem=send.at[i], recv_sem=recv.at[i],
            device_id={"expert": lax.rem(me + 1, owners)}, device_id_type=MESH,
        ).wait_send()

    split_frames(dy_ref, s0)
    langs_own = langs.at[0]
    langs_all = langs.at[1]

    def spread_langs(d, carry):
        langs_own[d] = lang_ref[...]
        return carry

    lax.fori_loop(0, owners, spread_langs, 0)
    pl.semaphore_wait(barrier, owners - 1 + shards - 1)
    scatter(langs_own, langs_all, 0)
    scatter(s0, r0, 1)
    split_frames(x_ref, s1)
    scatter(s1, r1, 2)

    for k in range(taps):
        tapb[k] = jnp.broadcast_to(taps_ref[k : k + 1, :].astype(F32), (segs, width))
    for pad in (gpad, spad):
        pad[:half] = jnp.zeros((half, segs, LANES), F32)
        pad[half + frames :] = jnp.zeros((pad.shape[0] - half - frames, segs, LANES), F32)

    arrived(langs_own, langs_all, 0)
    owner_of = lax.broadcasted_iota(jnp.int32, (owners, LANES), 0).astype(F32)
    before = lax.broadcasted_iota(jnp.int32, (LANES, LANES), 0) < lax.broadcasted_iota(
        jnp.int32, (LANES, LANES), 1
    )
    before = jnp.where(before, 1.0, 0.0).astype(BF16)
    place = lax.broadcasted_iota(jnp.int32, (total, LANES), 0).astype(F32)
    base = jnp.zeros((owners, 1), F32)
    group = LANES // segs
    for q in range(total // LANES):
        row = jnp.sum(langs_all[q * group : (q + 1) * group], axis=0)
        match = jnp.where(owner_of == row, 1.0, 0.0)
        rank = jnp.dot(match.astype(BF16), before, preferred_element_type=F32) + base
        base = base + jnp.sum(match, axis=1, keepdims=True)
        dest = jnp.sum(match * (owner_of * segs + rank), axis=0, keepdims=True)
        pick[:, q * LANES : (q + 1) * LANES] = jnp.where(place == dest, 1.0, 0.0).astype(BF16)
    number = lax.broadcasted_iota(jnp.int32, (16, total), 1)
    which = lax.broadcasted_iota(jnp.int32, (16, total), 0)
    digits = jnp.where(which == 0, number // 32, number % 32).astype(F32).astype(BF16)
    found = lax.dot_general(digits, pick[...], (((1,), (1,)), ((), ())), preferred_element_type=F32)
    source = found[0:1] * 32.0 + found[1:2]
    for q in range(total // LANES):
        cols = slice(q * LANES, (q + 1) * LANES)
        pick_t[:, cols] = jnp.where(place == source[:, cols], 1.0, 0.0).astype(BF16)

    def permute(chosen, src, dst):
        rows = 256

        def block(b, carry):
            choice = chosen[pl.ds(pl.multiple_of(b * rows, rows), rows), :]
            for j in range(2):
                flat = src[:, j].reshape(total, width)
                moved = jnp.dot(choice, flat, preferred_element_type=F32).astype(BF16)
                dst[pl.ds(b * (rows // segs), rows // segs), j] = moved.reshape(rows // segs, segs, width)
            return carry

        lax.fori_loop(0, total // rows, block, 0)

    arrived(s0, r0, 1)
    sent(s0, r0, 1)
    permute(pick, r0, s0)
    scatter(s0, dy_own, 3)
    arrived(s1, r1, 2)
    sent(s1, r1, 2)
    permute(pick, r1, s1)
    scatter(s1, x_own, 4)

    def ring_copy(src, dst, i, d):
        return pltpu.make_async_remote_copy(
            src_ref=src, dst_ref=dst, send_sem=ring_send.at[i], recv_sem=ring_recv.at[i],
            device_id={"fsdp": peer_x[d]}, device_id_type=MESH,
        )

    arrived(s0, dy_own, 3)
    up = ring_copy(dy_own, ring.at[0], 0, 1)
    down = ring_copy(dy_own, ring.at[1], 1, shards - 1)
    up.start()
    down.start()

    def exchange(src, dst, i):
        copies = [
            pltpu.make_async_remote_copy(
                src_ref=src, dst_ref=dst.at[d], send_sem=ex_send.at[i, d], recv_sem=ex_recv.at[i, d],
                device_id={"fsdp": peer_x[d]}, device_id_type=MESH,
            )
            for d in range(1, shards)
        ]
        for copy in copies:
            copy.start()
        return copies

    arrived(s1, x_own, 4)

    def moments(b, carry):
        x = x_own[pl.ds(b * (FB // 2), FB // 2)].astype(F32).reshape(FB, segs, width)
        mean = jnp.sum(x, axis=2, keepdims=True) * (1.0 / width)
        centre = x - mean
        square = jnp.sum(centre * centre, axis=2, keepdims=True)
        mom[0, pl.ds(pl.multiple_of(b * FB, FB), FB)] = to_row(mean, square, segs)
        return carry

    lax.fori_loop(0, frames // FB, moments, 0)
    copies = exchange(mom.at[0], parts, 0)
    up.wait_recv()
    down.wait_recv()
    middle = owners // 2
    up2 = ring_copy(ring.at[0, pl.ds(0, middle)], ring.at[2, pl.ds(0, middle)], 2, 1)
    down2 = ring_copy(ring.at[1, pl.ds(middle, middle)], ring.at[2, pl.ds(middle, middle)], 3, shards - 1)
    up2.start()
    down2.start()
    for copy in copies:
        copy.wait()

    def normalize(b, carry):
        at = pl.ds(pl.multiple_of(b * FB, FB), FB)
        rows = [mom[0, at]] + [parts[d, at] for d in range(1, shards)]
        mean, scale = mean_and_scale(rows, width)
        mean = to_column(mean, segs)
        scale = to_column(scale, segs)
        x = x_own[pl.ds(b * (FB // 2), FB // 2)].astype(F32).reshape(FB, segs, width)
        normed[at] = (x - mean) * scale
        scale_c[at] = jnp.broadcast_to(scale, (FB, segs, LANES))
        return carry

    lax.fori_loop(0, frames // FB, normalize, 0)

    def convolve(lb, carry):
        lanes = pl.ds(pl.multiple_of(lb * LANES, LANES), LANES)
        gain = gain_ref[:, lanes].astype(F32)

        def fill(i, c):
            at = pl.ds(i * FB, FB)
            spad[pl.ds(i * FB + half, FB)] = normed[at, :, lanes] * gain[None]
            return c

        lax.fori_loop(0, frames // FB, fill, 0)

        def step(i, c):
            t = i * STEP
            acc = tapb[0, :, lanes][None] * spad[pl.ds(t, STEP)]
            for k in range(1, taps):
                acc = acc + tapb[k, :, lanes][None] * spad[pl.ds(t + k, STEP)]
            conv[pl.ds(t, STEP), :, lanes] = acc
            hidden[pl.ds(t, STEP), :, lanes] = (acc / (1.0 + jnp.exp(-acc))).astype(BF16)
            return c

        lax.fori_loop(0, frames // STEP, step, 0)
        return carry

    lax.fori_loop(0, chunks, convolve, 0)

    up2.wait_recv()
    down2.wait_recv()

    def column(d):
        return pl.ds(pl.multiple_of(peer_x[d] * width, LANES), width)

    pieces = [(dy_own, 0), (ring.at[0], shards - 1), (ring.at[1], 1), (ring.at[2], 2)]

    def hid_block(b, carry):
        acc = None
        for piece, d in pieces:
            rows = piece[pl.ds(b * (FB // 2), FB // 2)].reshape(FB * segs, width)
            term = lax.dot_general(
                rows, w_ref[:, column(d)], (((1,), (1,)), ((), ())), preferred_element_type=F32
            )
            acc = term if acc is None else acc + term
        hid[pl.ds(b * FB, FB)] = acc.reshape(FB, segs, width)
        return carry

    lax.fori_loop(0, frames // FB, hid_block, 0)

    sum_a[...] = jnp.zeros_like(sum_a)
    sum_b[...] = jnp.zeros_like(sum_b)

    def backward(lb, carry):
        lanes = pl.ds(pl.multiple_of(lb * LANES, LANES), LANES)
        gain = gain_ref[:, lanes].astype(F32)

        def fill(i, c):
            at = pl.ds(i * STEP, STEP)
            a = conv[at, :, lanes]
            s = 1.0 / (1.0 + jnp.exp(-a))
            gpad[pl.ds(i * STEP + half, STEP)] = hid[at, :, lanes] * s * (1.0 + a * (1.0 - s))
            spad[pl.ds(i * STEP + half, STEP)] = normed[at, :, lanes] * gain[None]
            return c

        lax.fori_loop(0, frames // STEP, fill, 0)

        def transposed(i, gain_sum):
            t = i * STEP
            at = pl.ds(t, STEP)
            acc = tapb[0, :, lanes][None] * gpad[pl.ds(t + taps - 1, STEP)]
            for k in range(1, taps):
                acc = acc + tapb[k, :, lanes][None] * gpad[pl.ds(t + taps - 1 - k, STEP)]
            hid[at, :, lanes] = acc
            cross = acc * normed[at, :, lanes]
            sum_a[at] = sum_a[at] + acc * gain[None]
            sum_b[at] = sum_b[at] + cross * gain[None]
            return gain_sum + jnp.sum(cross, axis=0)

        gain_sum = lax.fori_loop(0, frames // STEP, transposed, jnp.zeros((segs, LANES), F32))
        ggrad_ref[:, lanes] = jnp.sum(gain_sum, axis=0, keepdims=True) * grad_scale
        kacc[...] = jnp.zeros_like(kacc)

        def tap_sums(i, c):
            t = i * STEP
            g = gpad[pl.ds(t + half, STEP)]
            for k in range(taps):
                kacc[k] = kacc[k] + jnp.sum(g * spad[pl.ds(t + k, STEP)], axis=0)
            return c

        lax.fori_loop(0, frames // STEP, tap_sums, 0)
        for k in range(taps):
            kgrad_ref[k : k + 1, lanes] = jnp.sum(kacc[k], axis=0, keepdims=True) * grad_scale
        return carry

    lax.fori_loop(0, chunks, backward, 0)

    def sum_rows(b, carry):
        at = pl.ds(pl.multiple_of(b * FB, FB), FB)
        first = jnp.sum(sum_a[at], axis=2, keepdims=True)
        second = jnp.sum(sum_b[at], axis=2, keepdims=True)
        mom[1, at] = to_row(first, second, segs)
        return carry

    lax.fori_loop(0, frames // FB, sum_rows, 0)
    copies = exchange(mom.at[1], sums, 1)
    sent(s0, dy_own, 3)
    for copy in copies:
        copy.wait()

    def finish(b, carry):
        at = pl.ds(pl.multiple_of(b * FB, FB), FB)
        row = mom[1, at]
        for d in range(1, shards):
            row = row + sums[d, at]
        row = row * (1.0 / (shards * width))
        plain = to_column(row, segs)
        cross = to_column(pltpu.roll(row, LANES // 2, 1), segs)
        scale = scale_c[at][:, :, 0:1]
        ng = hid[at] * gain_ref[...].astype(F32)[None]
        branch = scale * (ng - plain - normed[at] * cross)
        dy = dy_own[pl.ds(b * (FB // 2), FB // 2)].astype(F32).reshape(FB, segs, width)
        s0[pl.ds(b * (FB // 2), FB // 2)] = (dy + branch).astype(BF16).reshape(FB // 2, 2, segs, width)
        return carry

    lax.fori_loop(0, frames // FB, finish, 0)
    scatter(s0, r0, 5)

    hidden_rows = hidden[...].reshape(frames * segs, width)
    for piece, d in pieces:
        rows = piece[...].reshape(frames * segs, width)
        block = lax.dot_general(hidden_rows, rows, (((0,), (0,)), ((), ())), preferred_element_type=F32)
        wgrad_ref[:, column(d)] = (block * grad_scale).astype(BF16)

    sent(s1, x_own, 4)
    arrived(s0, r0, 5)
    permute(pick_t, r0, s1)
    scatter(s1, r1, 6)
    sent(langs_own, langs_all, 0)
    for copy in (up, down, up2, down2):
        copy.wait_send()
    sent(s0, r0, 5)
    arrived(s1, r1, 6)

    def join_frames(b, carry):
        rows = r1[pl.ds(b * (FB // 2), FB // 2)].astype(F32).reshape(FB, segs, width)
        feat_ref[:, pl.ds(pl.multiple_of(b * FB, FB), FB), :] = jnp.swapaxes(rows, 0, 1).astype(BF16)
        return carry

    lax.fori_loop(0, frames // FB, join_frames, 0)
    sent(s1, r1, 6)


def per_device(feats, cotan, lang, w_out, gain, kernel):
    segs, frames, width = feats.shape
    owners = lax.axis_size("expert")
    shards = lax.axis_size("fsdp")
    taps = kernel.shape[1]
    total = owners * segs
    grad_scale = float(segs * frames) ** (-0.5)
    group = LANES // segs
    lane_owner = jnp.arange(LANES, dtype=jnp.int32) // segs
    here = lane_owner == lax.axis_index("expert") % group
    lang_row = jnp.where(here, jnp.tile(lang, group), 0).astype(F32)[None, :]

    shape = jax.ShapeDtypeStruct
    blocks = (owners, frames // owners, segs, width)
    f32_rows = pltpu.VMEM((frames, segs, width), F32)
    columns = pltpu.VMEM((frames, segs, LANES), F32)
    padded = pltpu.VMEM((frames + 32, segs, LANES), F32)
    dma = pltpu.SemaphoreType.DMA
    vmem = pl.BlockSpec(memory_space=pltpu.VMEM)
    feat_grad, w_grad, gain_grad, tap_grad = pl.pallas_call(
        functools.partial(module_kernel, owners, shards, grad_scale),
        out_shape=(
            shape((segs, frames, width), BF16),
            shape(w_out.shape[1:], BF16),
            shape((1, width), F32),
            shape((taps, width), F32),
        ),
        in_specs=[vmem] * 6,
        out_specs=(vmem,) * 4,
        scratch_shapes=[
            pltpu.VMEM((2, owners, 1, LANES), F32),
            *[pltpu.VMEM(blocks, BF16)] * 6,
            pltpu.VMEM((shards - 1,) + blocks, BF16),
            pltpu.VMEM((total, total), BF16),
            pltpu.VMEM((total, total), BF16),
            f32_rows,
            f32_rows,
            pltpu.VMEM((frames, segs, width), BF16),
            f32_rows,
            padded,
            padded,
            pltpu.VMEM((taps, segs, width), F32),
            pltpu.VMEM((taps, segs, LANES), F32),
            columns,
            columns,
            columns,
            pltpu.VMEM((2, frames, LANES), F32),
            pltpu.VMEM((shards, frames, LANES), F32),
            pltpu.VMEM((shards, frames, LANES), F32),
            dma((7,)),
            dma((7,)),
            dma((4,)),
            dma((4,)),
            dma((2, shards)),
            dma((2, shards)),
        ],
        compiler_params=pltpu.CompilerParams(
            collective_id=0, has_side_effects=True, vmem_limit_bytes=67043328
        ),
        name="module_backward",
    )(lang_row, feats, cotan, w_out[0], gain, kernel[0])
    return feat_grad, w_grad[None], gain_grad, tap_grad[None]


def solution(mesh):
    in_specs = (
        P("expert", None, "fsdp"),
        P("expert", None, "fsdp"),
        P("expert"),
        P("expert", "fsdp", None),
        P("expert", "fsdp"),
        P("expert", None, "fsdp"),
    )
    out_specs = (
        P("expert", None, "fsdp"),
        P("expert", "fsdp", None),
        P("expert", "fsdp"),
        P("expert", None, "fsdp"),
    )
    return jax.shard_map(
        per_device, mesh=mesh, in_specs=in_specs, out_specs=out_specs, check_vma=False
    )
```

```python
import functools

import jax
import jax.numpy as jnp
from jax import lax
from jax.experimental import pallas as pl
from jax.experimental.pallas import tpu as pltpu
from jax.sharding import PartitionSpec as P

MESH = pl.DeviceIdType.MESH
F32 = jnp.float32
BF16 = jnp.bfloat16
LANES = 128
STEP = 16
FB = 16


def diagonal(segs):
    lane = lax.broadcasted_iota(jnp.int32, (1, segs, LANES), 2)
    seg = lax.broadcasted_iota(jnp.int32, (1, segs, LANES), 1)
    return lane == seg, lane == seg + segs


def to_row(first, second, segs):
    low, high = diagonal(segs)
    spread = jnp.where(low, first, 0.0) + jnp.where(high, second, 0.0)
    return jnp.sum(spread, axis=1)


def to_column(row, segs):
    low, _ = diagonal(segs)
    return jnp.sum(jnp.where(low, row[:, None, :], 0.0), axis=2, keepdims=True)


def mean_and_scale(rows, width, segs):
    n = len(rows)
    squares = [pltpu.roll(r, LANES - segs, 1) for r in rows]
    mean = sum(rows) * (1.0 / n)
    spread = sum((r - mean) * (r - mean) for r in rows)
    var = (sum(squares) + width * spread) * (1.0 / (n * width))
    return mean, lax.rsqrt(var + 1e-05)


def module_kernel(
    owners, shards, grad_scale,
    lang_ref, x_ref, dy_ref, w_ref, gain_ref, taps_ref,
    feat_ref, wgrad_ref, ggrad_ref, kgrad_ref,
    langs, s0, s1, r0, r1, p_dy, p_x, own_dy, own_x, ring, back, pick, pick_t,
    normed, conv, hidden, hid, gpad, spad, tapb, kacc, gacc, sum_a, sum_b, scale_c, rows_a, rows_b, mom, parts,
    send, recv, ring_send, ring_recv, ex_send, ex_recv,
):
    all_segs, frames, width = x_ref.shape
    segs = own_x.shape[3]
    taps = taps_ref.shape[0]
    half = taps // 2
    total = owners * all_segs
    part = owners * segs
    chunks = width // LANES
    blocks = frames // FB
    me = lax.axis_index("expert")
    fs = lax.axis_index("fsdp")
    peer_x = [lax.rem(fs + d, shards) for d in range(shards)]

    barrier = pltpu.get_barrier_semaphore()

    def greet(d, carry):
        pl.semaphore_signal(
            barrier, inc=1, device_id={"expert": lax.rem(me + d, owners)}, device_id_type=MESH
        )
        return carry

    lax.fori_loop(1, owners, greet, 0)
    for d in range(1, shards):
        pl.semaphore_signal(barrier, inc=1, device_id={"fsdp": peer_x[d]}, device_id_type=MESH)

    def split_frames(src, dst):
        def block(b, carry):
            rows = src[:, pl.ds(pl.multiple_of(b * FB, FB), FB), :].astype(F32)
            moved = jnp.swapaxes(rows, 0, 1).astype(BF16)
            dst[pl.ds(b * (FB // 2), FB // 2)] = moved.reshape(FB // 2, 2, all_segs, width)
            return carry

        lax.fori_loop(0, blocks, block, 0)

    def scatter(src, dst, i):
        def one(p):
            pltpu.make_async_remote_copy(
                src_ref=src.at[p], dst_ref=dst.at[me], send_sem=send.at[i], recv_sem=recv.at[i],
                device_id={"expert": p}, device_id_type=MESH,
            ).start()

        def both(d, carry):
            one(lax.rem(me + d, owners))
            one(lax.rem(me + owners - d, owners))
            return carry

        lax.fori_loop(1, owners // 2, both, 0)
        one(lax.rem(me + owners // 2, owners))
        pltpu.make_async_copy(src.at[me], dst.at[me], recv.at[i]).start()

    def arrived(src, dst, i):
        pltpu.make_async_copy(src, dst, recv.at[i]).wait()

    def sent(src, dst, i):
        most = pl.ds(0, owners - 1)
        pltpu.make_async_remote_copy(
            src_ref=src.at[most], dst_ref=dst.at[most], send_sem=send.at[i], recv_sem=recv.at[i],
            device_id={"expert": lax.rem(me + 1, owners)}, device_id_type=MESH,
        ).wait_send()

    split_frames(dy_ref, s0)
    langs_own = langs.at[0]
    langs_all = langs.at[1]

    def spread_langs(d, carry):
        langs_own[d] = lang_ref[...]
        return carry

    lax.fori_loop(0, owners, spread_langs, 0)
    pl.semaphore_wait(barrier, owners - 1 + shards - 1)
    scatter(langs_own, langs_all, 0)
    scatter(s0, r0, 1)
    split_frames(x_ref, s1)
    scatter(s1, r1, 2)

    for k in range(taps):
        tapb[k] = jnp.broadcast_to(taps_ref[k : k + 1, :].astype(F32), (segs, width))
    for pad in (gpad, spad):
        pad[:half] = jnp.zeros((half, segs, LANES), F32)
        pad[half + frames :] = jnp.zeros((pad.shape[0] - half - frames, segs, LANES), F32)
    kacc[...] = jnp.zeros_like(kacc)
    gacc[...] = jnp.zeros_like(gacc)

    arrived(langs_own, langs_all, 0)
    owner_of = lax.broadcasted_iota(jnp.int32, (owners, LANES), 0).astype(F32)
    before = lax.broadcasted_iota(jnp.int32, (LANES, LANES), 0) < lax.broadcasted_iota(
        jnp.int32, (LANES, LANES), 1
    )
    before = jnp.where(before, 1.0, 0.0).astype(BF16)
    place = lax.broadcasted_iota(jnp.int32, (total, LANES), 0).astype(F32)
    base = jnp.zeros((owners, 1), F32)
    group = LANES // all_segs
    for q in range(total // LANES):
        row = jnp.sum(langs_all[q * group : (q + 1) * group], axis=0)
        match = jnp.where(owner_of == row, 1.0, 0.0)
        rank = jnp.dot(match.astype(BF16), before, preferred_element_type=F32) + base
        base = base + jnp.sum(match, axis=1, keepdims=True)
        spot = owner_of * segs + rank + jnp.where(rank >= segs, float(part - segs), 0.0)
        dest = jnp.sum(match * spot, axis=0, keepdims=True)
        pick[:, q * LANES : (q + 1) * LANES] = jnp.where(place == dest, 1.0, 0.0).astype(BF16)
    number = lax.broadcasted_iota(jnp.int32, (16, total), 1)
    which = lax.broadcasted_iota(jnp.int32, (16, total), 0)
    digits = jnp.where(which == 0, number // 32, number % 32).astype(F32).astype(BF16)
    found = lax.dot_general(digits, pick[...], (((1,), (1,)), ((), ())), preferred_element_type=F32)
    source = found[0:1] * 32.0 + found[1:2]
    for q in range(total // LANES):
        cols = slice(q * LANES, (q + 1) * LANES)
        pick_t[:, cols] = jnp.where(place == source[:, cols], 1.0, 0.0).astype(BF16)

    def permute_out(h, src, dst):
        rows = 256

        def block(b, carry):
            choice = pick[pl.ds(pl.multiple_of(h * part + b * rows, rows), rows), :]
            for j in range(2):
                flat = src[:, j].reshape(total, width)
                moved = jnp.dot(choice, flat, preferred_element_type=F32).astype(BF16)
                dst[pl.ds(b * (rows // segs), rows // segs), j] = moved.reshape(rows // segs, segs, width)
            return carry

        lax.fori_loop(0, part // rows, block, 0)

    def permute_home(dst):
        rows = 256

        def block(b, carry):
            at = pl.ds(pl.multiple_of(b * rows, rows), rows)
            for j in range(2):
                moved = None
                for h in range(2):
                    flat = back[h, :, j].reshape(part, width)
                    term = jnp.dot(pick_t[at, h * part : (h + 1) * part], flat, preferred_element_type=F32)
                    moved = term if moved is None else moved + term
                moved = moved.astype(BF16).reshape(rows // all_segs, all_segs, width)
                dst[pl.ds(b * (rows // all_segs), rows // all_segs), j] = moved
            return carry

        lax.fori_loop(0, total // rows, block, 0)

    arrived(s0, r0, 1)
    permute_out(0, r0, p_dy.at[0])
    scatter(p_dy.at[0], own_dy.at[0], 3)
    permute_out(1, r0, p_dy.at[1])
    arrived(s1, r1, 2)
    permute_out(0, r1, p_x.at[0])
    scatter(p_x.at[0], own_x.at[0], 4)
    scatter(p_dy.at[1], own_dy.at[1], 5)
    permute_out(1, r1, p_x.at[1])
    scatter(p_x.at[1], own_x.at[1], 6)

    def ring_copy(h, src, dst, i, d):
        return pltpu.make_async_remote_copy(
            src_ref=src, dst_ref=dst, send_sem=ring_send.at[h, i], recv_sem=ring_recv.at[h, i],
            device_id={"fsdp": peer_x[d]}, device_id_type=MESH,
        )

    middle = owners // 2

    def ring_copies(h):
        one = ring.at[h, 0]
        two = ring.at[h, 1]
        far = ring.at[h, 2]
        low = pl.ds(0, middle)
        high = pl.ds(middle, middle)
        return [
            ring_copy(h, own_dy.at[h], one, 0, 1),
            ring_copy(h, own_dy.at[h], two, 1, shards - 1),
            ring_copy(h, one.at[low], far.at[low], 2, 1),
            ring_copy(h, two.at[high], far.at[high], 3, shards - 1),
        ]

    rings = [ring_copies(0), ring_copies(1)]

    def start_ring(h):
        arrived(p_dy.at[h], own_dy.at[h], 3 + 2 * h)
        rings[h][0].start()
        rings[h][1].start()

    def exchange(i):
        copies = [
            pltpu.make_async_remote_copy(
                src_ref=mom.at[i], dst_ref=parts.at[i, d], send_sem=ex_send.at[i, d],
                recv_sem=ex_recv.at[i, d], device_id={"fsdp": peer_x[d]}, device_id_type=MESH,
            )
            for d in range(1, shards)
        ]
        for copy in copies:
            copy.start()
        return copies

    def gathered(i):
        return [mom[i]] + [parts[i, d] for d in range(1, shards)]

    def pack():
        packed = rows_a[0]
        for b in range(1, blocks):
            packed = packed + pltpu.roll(rows_a[b], 2 * segs * b, 1)
        return packed

    def unpack(packed, dst):
        dst[0] = packed
        for b in range(1, blocks):
            dst[b] = pltpu.roll(packed, LANES - 2 * segs * b, 1)

    def column(d):
        return pl.ds(pl.multiple_of(peer_x[d] * width, LANES), width)

    def pieces(h):
        return [
            (own_dy.at[h], 0), (ring.at[h, 0], shards - 1), (ring.at[h, 1], 1), (ring.at[h, 2], 2)
        ]

    def stage(h, between):
        dy = own_dy.at[h]
        x_own = own_x.at[h]
        arrived(p_x.at[h], x_own, 4 + 2 * h)

        def moments(b, carry):
            x = x_own[pl.ds(b * (FB // 2), FB // 2)].astype(F32).reshape(FB, segs, width)
            mean = jnp.sum(x, axis=2, keepdims=True) * (1.0 / width)
            centre = x - mean
            square = jnp.sum(centre * centre, axis=2, keepdims=True)
            rows_a[b] = to_row(mean, square, segs)
            return carry

        lax.fori_loop(0, blocks, moments, 0)
        mom[2 * h] = pack()
        copies = exchange(2 * h)
        up, down, up2, down2 = rings[h]
        up.wait_recv()
        down.wait_recv()
        up2.start()
        down2.start()
        for copy in copies:
            copy.wait()
        mean_row, scale_row = mean_and_scale(gathered(2 * h), width, segs)
        unpack(mean_row, rows_a)
        unpack(scale_row, rows_b)

        def normalize(b, carry):
            at = pl.ds(b * FB, FB)
            mean = to_column(rows_a[b], segs)
            scale = to_column(rows_b[b], segs)
            x = x_own[pl.ds(b * (FB // 2), FB // 2)].astype(F32).reshape(FB, segs, width)
            normed[at] = (x - mean) * scale
            scale_c[at] = jnp.broadcast_to(scale, (FB, segs, LANES))
            return carry

        lax.fori_loop(0, blocks, normalize, 0)

        def convolve(lb, carry):
            lanes = pl.ds(pl.multiple_of(lb * LANES, LANES), LANES)
            gain = gain_ref[:, lanes].astype(F32)

            def fill(i, c):
                at = pl.ds(i * FB, FB)
                spad[pl.ds(i * FB + half, FB)] = normed[at, :, lanes] * gain[None]
                return c

            lax.fori_loop(0, blocks, fill, 0)

            def step(i, c):
                t = i * STEP
                acc = tapb[0, :, lanes][None] * spad[pl.ds(t, STEP)]
                for k in range(1, taps):
                    acc = acc + tapb[k, :, lanes][None] * spad[pl.ds(t + k, STEP)]
                conv[pl.ds(t, STEP), :, lanes] = acc
                hidden[h, pl.ds(t, STEP), :, lanes] = (acc / (1.0 + jnp.exp(-acc))).astype(BF16)
                return c

            lax.fori_loop(0, frames // STEP, step, 0)
            return carry

        lax.fori_loop(0, chunks, convolve, 0)
        up2.wait_recv()
        down2.wait_recv()

        def hid_block(b, carry):
            acc = None
            for piece, d in pieces(h):
                rows = piece[pl.ds(b * FB, FB)].reshape(2 * FB * segs, width)
                term = lax.dot_general(
                    rows, w_ref[:, column(d)], (((1,), (1,)), ((), ())), preferred_element_type=F32
                )
                acc = term if acc is None else acc + term
            hid[pl.ds(b * 2 * FB, 2 * FB)] = acc.reshape(2 * FB, segs, width)
            return carry

        lax.fori_loop(0, blocks // 2, hid_block, 0)
        sum_a[...] = jnp.zeros_like(sum_a)
        sum_b[...] = jnp.zeros_like(sum_b)

        def backward(lb, carry):
            lanes = pl.ds(pl.multiple_of(lb * LANES, LANES), LANES)
            gain = gain_ref[:, lanes].astype(F32)

            def fill(i, c):
                at = pl.ds(i * STEP, STEP)
                a = conv[at, :, lanes]
                s = 1.0 / (1.0 + jnp.exp(-a))
                gpad[pl.ds(i * STEP + half, STEP)] = hid[at, :, lanes] * s * (1.0 + a * (1.0 - s))
                spad[pl.ds(i * STEP + half, STEP)] = normed[at, :, lanes] * gain[None]
                return c

            lax.fori_loop(0, frames // STEP, fill, 0)

            def transposed(i, gain_sum):
                t = i * STEP
                at = pl.ds(t, STEP)
                acc = tapb[0, :, lanes][None] * gpad[pl.ds(t + taps - 1, STEP)]
                for k in range(1, taps):
                    acc = acc + tapb[k, :, lanes][None] * gpad[pl.ds(t + taps - 1 - k, STEP)]
                hid[at, :, lanes] = acc
                cross = acc * normed[at, :, lanes]
                sum_a[at] = sum_a[at] + acc * gain[None]
                sum_b[at] = sum_b[at] + cross * gain[None]
                return gain_sum + jnp.sum(cross, axis=0)

            zero = jnp.zeros((segs, LANES), F32)
            gacc[:, lanes] = gacc[:, lanes] + lax.fori_loop(0, frames // STEP, transposed, zero)

            def tap_sums(i, c):
                t = i * STEP
                g = gpad[pl.ds(t + half, STEP)]
                for k in range(taps):
                    kacc[k, :, lanes] = kacc[k, :, lanes] + jnp.sum(g * spad[pl.ds(t + k, STEP)], axis=0)
                return c

            lax.fori_loop(0, frames // STEP, tap_sums, 0)
            return carry

        lax.fori_loop(0, chunks - 1, backward, 0)
        between()
        lax.fori_loop(chunks - 1, chunks, backward, 0)

        def sum_rows(b, carry):
            at = pl.ds(b * FB, FB)
            first = jnp.sum(sum_a[at], axis=2, keepdims=True)
            second = jnp.sum(sum_b[at], axis=2, keepdims=True)
            rows_a[b] = to_row(first, second, segs)
            return carry

        lax.fori_loop(0, blocks, sum_rows, 0)
        mom[2 * h + 1] = pack()
        copies = exchange(2 * h + 1)
        sent(p_dy.at[h], dy, 3 + 2 * h)
        for copy in copies:
            copy.wait()
        row = sum(gathered(2 * h + 1)) * (1.0 / (shards * width))
        unpack(row, rows_a)
        unpack(pltpu.roll(row, LANES - segs, 1), rows_b)

        def finish(b, carry):
            at = pl.ds(b * FB, FB)
            plain = to_column(rows_a[b], segs)
            cross = to_column(rows_b[b], segs)
            scale = scale_c[at][:, :, 0:1]
            ng = hid[at] * gain_ref[...].astype(F32)[None]
            branch = scale * (ng - plain - normed[at] * cross)
            grads = dy[pl.ds(b * (FB // 2), FB // 2)].astype(F32).reshape(FB, segs, width)
            p_dy[h, pl.ds(b * (FB // 2), FB // 2)] = (
                (grads + branch).astype(BF16).reshape(FB // 2, 2, segs, width)
            )
            return carry

        lax.fori_loop(0, blocks, finish, 0)
        scatter(p_dy.at[h], back.at[h], 7 + h)

    start_ring(0)
    stage(0, lambda: start_ring(1))
    stage(1, lambda: None)

    for k in range(taps):
        kgrad_ref[k] = jnp.sum(kacc[k], axis=0, keepdims=True) * grad_scale
    ggrad_ref[...] = jnp.sum(gacc[...], axis=0, keepdims=True) * grad_scale
    rows_of = frames * segs
    for j in range(shards):
        block = None
        for h in range(2):
            piece, d = pieces(h)[j]
            term = lax.dot_general(
                hidden[h].reshape(rows_of, width), piece[...].reshape(rows_of, width),
                (((0,), (0,)), ((), ())), preferred_element_type=F32,
            )
            block = term if block is None else block + term
        wgrad_ref[:, column(d)] = (block * grad_scale).astype(BF16)

    sent(s0, r0, 1)
    arrived(p_dy.at[0], back.at[0], 7)
    arrived(p_dy.at[1], back.at[1], 8)
    permute_home(s0)
    scatter(s0, r0, 9)
    sent(langs_own, langs_all, 0)
    sent(s1, r1, 2)
    for h in range(2):
        sent(p_x.at[h], own_x.at[h], 4 + 2 * h)
        sent(p_dy.at[h], back.at[h], 7 + h)
        for copy in rings[h]:
            copy.wait_send()
    arrived(s0, r0, 9)

    def join_frames(b, carry):
        rows = r0[pl.ds(b * (FB // 2), FB // 2)].astype(F32).reshape(FB, all_segs, width)
        feat_ref[:, pl.ds(pl.multiple_of(b * FB, FB), FB), :] = jnp.swapaxes(rows, 0, 1).astype(BF16)
        return carry

    lax.fori_loop(0, blocks, join_frames, 0)
    sent(s0, r0, 9)


def per_device(feats, cotan, lang, w_out, gain, kernel):
    segs, frames, width = feats.shape
    owners = lax.axis_size("expert")
    shards = lax.axis_size("fsdp")
    taps = kernel.shape[1]
    total = owners * segs
    grad_scale = float(segs * frames) ** (-0.5)
    group = LANES // segs
    lane_owner = jnp.arange(LANES, dtype=jnp.int32) // segs
    here = lane_owner == lax.axis_index("expert") % group
    lang_row = jnp.where(here, jnp.tile(lang, group), 0).astype(F32)[None, :]

    shape = jax.ShapeDtypeStruct
    half = segs // 2
    whole = pltpu.VMEM((owners, frames // owners, segs, width), BF16)
    halves = (owners, frames // owners, half, width)
    f32_rows = pltpu.VMEM((frames, half, width), F32)
    columns = pltpu.VMEM((frames, half, LANES), F32)
    padded = pltpu.VMEM((frames + 32, half, LANES), F32)
    rows = pltpu.VMEM((frames // FB, FB, LANES), F32)
    dma = pltpu.SemaphoreType.DMA
    vmem = pl.BlockSpec(memory_space=pltpu.VMEM)
    feat_grad, w_grad, gain_grad, tap_grad = pl.pallas_call(
        functools.partial(module_kernel, owners, shards, grad_scale),
        out_shape=(
            shape((segs, frames, width), BF16),
            shape(w_out.shape[1:], BF16),
            shape((1, width), F32),
            shape((taps, 1, width), F32),
        ),
        in_specs=[vmem] * 6,
        out_specs=(vmem,) * 4,
        scratch_shapes=[
            pltpu.VMEM((2, owners, 1, LANES), F32),
            *[whole] * 4,
            *[pltpu.VMEM((2,) + halves, BF16)] * 4,
            pltpu.VMEM((2, shards - 1) + halves, BF16),
            pltpu.VMEM((2,) + halves, BF16),
            pltpu.VMEM((total, total), BF16),
            pltpu.VMEM((total, total), BF16),
            f32_rows,
            f32_rows,
            pltpu.VMEM((2, frames, half, width), BF16),
            f32_rows,
            padded,
            padded,
            pltpu.VMEM((taps, half, width), F32),
            pltpu.VMEM((taps, half, width), F32),
            pltpu.VMEM((half, width), F32),
            columns,
            columns,
            columns,
            rows,
            rows,
            pltpu.VMEM((4, FB, LANES), F32),
            pltpu.VMEM((4, shards, FB, LANES), F32),
            dma((10,)),
            dma((10,)),
            dma((2, 4)),
            dma((2, 4)),
            dma((4, shards)),
            dma((4, shards)),
        ],
        compiler_params=pltpu.CompilerParams(
            collective_id=0, has_side_effects=True, vmem_limit_bytes=67043328
        ),
        name="module_backward",
    )(lang_row, feats, cotan, w_out[0], gain, kernel[0])
    return feat_grad, w_grad[None], gain_grad, jnp.swapaxes(tap_grad, 0, 1)


def solution(mesh):
    in_specs = (
        P("expert", None, "fsdp"),
        P("expert", None, "fsdp"),
        P("expert"),
        P("expert", "fsdp", None),
        P("expert", "fsdp"),
        P("expert", None, "fsdp"),
    )
    out_specs = (
        P("expert", None, "fsdp"),
        P("expert", "fsdp", None),
        P("expert", "fsdp"),
        P("expert", None, "fsdp"),
    )
    return jax.shard_map(
        per_device, mesh=mesh, in_specs=in_specs, out_specs=out_specs, check_vma=False
    )
```

```python
import functools

import jax
import jax.numpy as jnp
from jax import lax
from jax.experimental import pallas as pl
from jax.experimental.pallas import tpu as pltpu
from jax.sharding import PartitionSpec as P

MESH = pl.DeviceIdType.MESH
F32 = jnp.float32
BF16 = jnp.bfloat16
LANES = 128
STEP = 16
FB = 16


def diagonal(segs):
    lane = lax.broadcasted_iota(jnp.int32, (1, segs, LANES), 2)
    seg = lax.broadcasted_iota(jnp.int32, (1, segs, LANES), 1)
    return lane == seg, lane == seg + segs


def to_row(first, second, segs):
    low, high = diagonal(segs)
    spread = jnp.where(low, first, 0.0) + jnp.where(high, second, 0.0)
    return jnp.sum(spread, axis=1)


def to_column(row, segs):
    low, _ = diagonal(segs)
    return jnp.sum(jnp.where(low, row[:, None, :], 0.0), axis=2, keepdims=True)


def mean_and_scale(rows, width, segs):
    n = len(rows)
    squares = [pltpu.roll(r, LANES - segs, 1) for r in rows]
    mean = sum(rows) * (1.0 / n)
    spread = sum((r - mean) * (r - mean) for r in rows)
    var = (sum(squares) + width * spread) * (1.0 / (n * width))
    return mean, lax.rsqrt(var + 1e-05)


def module_kernel(
    owners, shards, grad_scale,
    lang_ref, x_ref, dy_ref, w_ref, gain_ref, taps_ref,
    home_ref, wgrad_ref, ggrad_ref, kgrad_ref,
    x_vmem, dy_vmem, w_vmem, langs, s0, s1, r0, r1, p_dy, p_x, own_dy, own_x, ring, ret, back, home, pick, pick_t,
    normed, conv, hidden, hid, gpad, spad, tapb, kacc, gacc, sum_a, sum_b, scale_c, rows_a, rows_b, mom, parts,
    send, recv, ring_send, ring_recv, ex_send, ex_recv, load,
):
    all_segs, frames, width = x_ref.shape
    segs = own_x.shape[3]
    taps = taps_ref.shape[0]
    half = taps // 2
    total = owners * all_segs
    part = owners * segs
    chunks = width // LANES
    blocks = frames // FB
    me = lax.axis_index("expert")
    fs = lax.axis_index("fsdp")
    peer_x = [lax.rem(fs + d, shards) for d in range(shards)]

    barrier = pltpu.get_barrier_semaphore()

    def greet(d, carry):
        pl.semaphore_signal(
            barrier, inc=1, device_id={"expert": lax.rem(me + d, owners)}, device_id_type=MESH
        )
        return carry

    loads = [
        pltpu.make_async_copy(src, dst, load.at[i])
        for i, (src, dst) in enumerate(((dy_ref, dy_vmem), (x_ref, x_vmem), (w_ref, w_vmem)))
    ]
    for copy in loads:
        copy.start()
    lax.fori_loop(1, owners, greet, 0)
    for d in range(1, shards):
        pl.semaphore_signal(barrier, inc=1, device_id={"fsdp": peer_x[d]}, device_id_type=MESH)

    def split_frames(src, dst):
        def block(b, carry):
            rows = src[:, pl.ds(pl.multiple_of(b * FB, FB), FB), :].astype(F32)
            moved = jnp.swapaxes(rows, 0, 1).astype(BF16)
            dst[pl.ds(b * (FB // 2), FB // 2)] = moved.reshape(FB // 2, 2, all_segs, width)
            return carry

        lax.fori_loop(0, blocks, block, 0)

    def scatter(src, dst, i):
        def one(p):
            pltpu.make_async_remote_copy(
                src_ref=src.at[p], dst_ref=dst.at[me], send_sem=send.at[i], recv_sem=recv.at[i],
                device_id={"expert": p}, device_id_type=MESH,
            ).start()

        def both(d, carry):
            one(lax.rem(me + d, owners))
            one(lax.rem(me + owners - d, owners))
            return carry

        lax.fori_loop(1, owners // 2, both, 0)
        one(lax.rem(me + owners // 2, owners))
        pltpu.make_async_copy(src.at[me], dst.at[me], recv.at[i]).start()

    def arrived(src, dst, i):
        pltpu.make_async_copy(src, dst, recv.at[i]).wait()

    def sent(src, dst, i):
        most = pl.ds(0, owners - 1)
        pltpu.make_async_remote_copy(
            src_ref=src.at[most], dst_ref=dst.at[most], send_sem=send.at[i], recv_sem=recv.at[i],
            device_id={"expert": lax.rem(me + 1, owners)}, device_id_type=MESH,
        ).wait_send()

    lane = lax.broadcasted_iota(jnp.int32, (1, LANES), 1)
    first_lane = lax.rem(me, LANES // all_segs) * all_segs
    lang_row = jnp.zeros((1, LANES), jnp.int32)
    for i in range(all_segs):
        lang_row = jnp.where(lane == first_lane + i, lang_ref[i], lang_row)
    lang_row = lang_row.astype(F32)
    loads[0].wait()
    split_frames(dy_vmem, s0)
    langs_own = langs.at[0]
    langs_all = langs.at[1]

    def spread_langs(d, carry):
        langs_own[d] = lang_row
        return carry

    lax.fori_loop(0, owners, spread_langs, 0)
    pl.semaphore_wait(barrier, owners - 1 + shards - 1)
    scatter(langs_own, langs_all, 0)
    scatter(s0, r0, 1)
    loads[1].wait()
    split_frames(x_vmem, s1)
    scatter(s1, r1, 2)

    for k in range(taps):
        tapb[k] = jnp.broadcast_to(taps_ref[k : k + 1, :].astype(F32), (segs, width))
    for pad in (gpad, spad):
        pad[:half] = jnp.zeros((half, segs, LANES), F32)
        pad[half + frames :] = jnp.zeros((pad.shape[0] - half - frames, segs, LANES), F32)
    kacc[...] = jnp.zeros_like(kacc)
    gacc[...] = jnp.zeros_like(gacc)

    arrived(langs_own, langs_all, 0)
    owner_of = lax.broadcasted_iota(jnp.int32, (owners, LANES), 0).astype(F32)
    before = lax.broadcasted_iota(jnp.int32, (LANES, LANES), 0) < lax.broadcasted_iota(
        jnp.int32, (LANES, LANES), 1
    )
    before = jnp.where(before, 1.0, 0.0).astype(BF16)
    place = lax.broadcasted_iota(jnp.int32, (total, LANES), 0).astype(F32)
    base = jnp.zeros((owners, 1), F32)
    group = LANES // all_segs
    for q in range(total // LANES):
        row = jnp.sum(langs_all[q * group : (q + 1) * group], axis=0)
        match = jnp.where(owner_of == row, 1.0, 0.0)
        rank = jnp.dot(match.astype(BF16), before, preferred_element_type=F32) + base
        base = base + jnp.sum(match, axis=1, keepdims=True)
        spot = owner_of * segs + rank + jnp.where(rank >= segs, float(part - segs), 0.0)
        dest = jnp.sum(match * spot, axis=0, keepdims=True)
        pick[:, q * LANES : (q + 1) * LANES] = jnp.where(place == dest, 1.0, 0.0).astype(BF16)
    number = lax.broadcasted_iota(jnp.int32, (16, total), 1)
    which = lax.broadcasted_iota(jnp.int32, (16, total), 0)
    digits = jnp.where(which == 0, number // 32, number % 32).astype(F32).astype(BF16)
    found = lax.dot_general(digits, pick[...], (((1,), (1,)), ((), ())), preferred_element_type=F32)
    source = found[0:1] * 32.0 + found[1:2]
    for q in range(total // LANES):
        cols = slice(q * LANES, (q + 1) * LANES)
        pick_t[:, cols] = jnp.where(place == source[:, cols], 1.0, 0.0).astype(BF16)

    def permute_out(h, src, dst):
        rows = 256

        def block(b, carry):
            choice = pick[pl.ds(pl.multiple_of(h * part + b * rows, rows), rows), :]
            for j in range(2):
                flat = src[:, j].reshape(total, width)
                moved = jnp.dot(choice, flat, preferred_element_type=F32).astype(BF16)
                dst[pl.ds(b * (rows // segs), rows // segs), j] = moved.reshape(rows // segs, segs, width)
            return carry

        lax.fori_loop(0, part // rows, block, 0)

    def permute_home(j, dst):
        rows = 256

        def block(b, carry):
            at = pl.ds(pl.multiple_of(b * rows, rows), rows)
            moved = None
            for h in range(2):
                flat = back[h, j].reshape(part, width)
                term = jnp.dot(pick_t[at, h * part : (h + 1) * part], flat, preferred_element_type=F32)
                moved = term if moved is None else moved + term
            moved = moved.astype(BF16).reshape(rows // all_segs, all_segs, width)
            dst[pl.ds(b * (rows // all_segs), rows // all_segs)] = moved
            return carry

        lax.fori_loop(0, total // rows, block, 0)

    arrived(s0, r0, 1)
    permute_out(0, r0, p_dy.at[0])
    scatter(p_dy.at[0], own_dy.at[0], 3)
    permute_out(1, r0, p_dy.at[1])
    arrived(s1, r1, 2)
    permute_out(0, r1, p_x.at[0])
    scatter(p_x.at[0], own_x.at[0], 4)
    scatter(p_dy.at[1], own_dy.at[1], 5)
    permute_out(1, r1, p_x.at[1])
    scatter(p_x.at[1], own_x.at[1], 6)

    def ring_copy(h, src, dst, i, d):
        return pltpu.make_async_remote_copy(
            src_ref=src, dst_ref=dst, send_sem=ring_send.at[h, i], recv_sem=ring_recv.at[h, i],
            device_id={"fsdp": peer_x[d]}, device_id_type=MESH,
        )

    middle = owners // 2

    def ring_copies(h):
        own = own_dy.at[h]
        one = ring.at[h, 0]
        two = ring.at[h, 1]
        far = ring.at[h, 2]
        low = pl.ds(0, middle)
        high = pl.ds(middle, middle)
        return [
            ring_copy(h, own.at[low], one.at[low], 0, 1),
            ring_copy(h, own.at[high], two.at[high], 1, shards - 1),
            ring_copy(h, own.at[high], one.at[high], 2, 1),
            ring_copy(h, own.at[low], two.at[low], 3, shards - 1),
            ring_copy(h, one.at[low], far.at[low], 4, 1),
            ring_copy(h, two.at[high], far.at[high], 5, shards - 1),
        ]

    rings = [ring_copies(0), ring_copies(1)]

    def start_ring(h):
        arrived(p_dy.at[h], own_dy.at[h], 3 + 2 * h)
        rings[h][0].start()
        rings[h][1].start()

    def go_on_ring(h):
        rings[h][2].start()
        rings[h][3].start()

    def exchange(i):
        copies = [
            pltpu.make_async_remote_copy(
                src_ref=mom.at[i], dst_ref=parts.at[i, d], send_sem=ex_send.at[i, d],
                recv_sem=ex_recv.at[i, d], device_id={"fsdp": peer_x[d]}, device_id_type=MESH,
            )
            for d in range(1, shards)
        ]
        for copy in copies:
            copy.start()
        return copies

    def gathered(i):
        return [mom[i]] + [parts[i, d] for d in range(1, shards)]

    def pack():
        packed = rows_a[0]
        for b in range(1, blocks):
            packed = packed + pltpu.roll(rows_a[b], 2 * segs * b, 1)
        return packed

    def unpack(packed, dst):
        dst[0] = packed
        for b in range(1, blocks):
            dst[b] = pltpu.roll(packed, LANES - 2 * segs * b, 1)

    def column(d):
        return pl.ds(pl.multiple_of(peer_x[d] * width, LANES), width)

    def pieces(h):
        return [
            (own_dy.at[h], 0), (ring.at[h, 0], shards - 1), (ring.at[h, 1], 1), (ring.at[h, 2], 2)
        ]

    def stage(h, between, after):
        dy = own_dy.at[h]
        x_own = own_x.at[h]
        arrived(p_x.at[h], x_own, 4 + 2 * h)

        def moments(b, carry):
            x = x_own[pl.ds(b * (FB // 2), FB // 2)].astype(F32).reshape(FB, segs, width)
            mean = jnp.sum(x, axis=2, keepdims=True) * (1.0 / width)
            centre = x - mean
            square = jnp.sum(centre * centre, axis=2, keepdims=True)
            rows_a[b] = to_row(mean, square, segs)
            return carry

        lax.fori_loop(0, blocks, moments, 0)
        mom[2 * h] = pack()
        copies = exchange(2 * h)
        for copy in rings[h][:4]:
            copy.wait_recv()
        rings[h][4].start()
        rings[h][5].start()

        def hid_rows(b, chosen):
            acc = None
            for piece, d in chosen:
                rows = piece[pl.ds(b * FB, FB)].reshape(2 * FB * segs, width)
                term = lax.dot_general(
                    rows, w_vmem[:, column(d)], (((1,), (1,)), ((), ())), preferred_element_type=F32
                )
                acc = term if acc is None else acc + term
            return acc.reshape(2 * FB, segs, width)

        def hid_near(b, carry):
            hid[pl.ds(b * 2 * FB, 2 * FB)] = hid_rows(b, pieces(h)[:3])
            return carry

        def hid_far(b, carry):
            at = pl.ds(b * 2 * FB, 2 * FB)
            hid[at] = hid[at] + hid_rows(b, pieces(h)[3:])
            return carry

        lax.fori_loop(0, blocks // 2, hid_near, 0)
        for copy in copies:
            copy.wait()
        mean_row, scale_row = mean_and_scale(gathered(2 * h), width, segs)
        unpack(mean_row, rows_a)
        unpack(scale_row, rows_b)

        def normalize(b, carry):
            at = pl.ds(b * FB, FB)
            mean = to_column(rows_a[b], segs)
            scale = to_column(rows_b[b], segs)
            x = x_own[pl.ds(b * (FB // 2), FB // 2)].astype(F32).reshape(FB, segs, width)
            normed[at] = (x - mean) * scale
            scale_c[at] = jnp.broadcast_to(scale, (FB, segs, LANES))
            return carry

        lax.fori_loop(0, blocks, normalize, 0)

        def convolve(lb, carry):
            lanes = pl.ds(pl.multiple_of(lb * LANES, LANES), LANES)
            gain = gain_ref[:, lanes].astype(F32)

            def fill(i, c):
                at = pl.ds(i * FB, FB)
                spad[pl.ds(i * FB + half, FB)] = normed[at, :, lanes] * gain[None]
                return c

            lax.fori_loop(0, blocks, fill, 0)

            def step(i, c):
                t = i * STEP
                acc = tapb[0, :, lanes][None] * spad[pl.ds(t, STEP)]
                for k in range(1, taps):
                    acc = acc + tapb[k, :, lanes][None] * spad[pl.ds(t + k, STEP)]
                conv[pl.ds(t, STEP), :, lanes] = acc
                hidden[h, pl.ds(t, STEP), :, lanes] = (acc / (1.0 + jnp.exp(-acc))).astype(BF16)
                return c

            lax.fori_loop(0, frames // STEP, step, 0)
            return carry

        lax.fori_loop(0, chunks, convolve, 0)
        rings[h][4].wait_recv()
        rings[h][5].wait_recv()
        lax.fori_loop(0, blocks // 2, hid_far, 0)
        between()
        sum_a[...] = jnp.zeros_like(sum_a)
        sum_b[...] = jnp.zeros_like(sum_b)

        def backward(lb, carry):
            lanes = pl.ds(pl.multiple_of(lb * LANES, LANES), LANES)
            gain = gain_ref[:, lanes].astype(F32)

            def fill(i, c):
                at = pl.ds(i * STEP, STEP)
                a = conv[at, :, lanes]
                s = 1.0 / (1.0 + jnp.exp(-a))
                gpad[pl.ds(i * STEP + half, STEP)] = hid[at, :, lanes] * s * (1.0 + a * (1.0 - s))
                spad[pl.ds(i * STEP + half, STEP)] = normed[at, :, lanes] * gain[None]
                return c

            lax.fori_loop(0, frames // STEP, fill, 0)

            def transposed(i, gain_sum):
                t = i * STEP
                at = pl.ds(t, STEP)
                acc = tapb[0, :, lanes][None] * gpad[pl.ds(t + taps - 1, STEP)]
                for k in range(1, taps):
                    acc = acc + tapb[k, :, lanes][None] * gpad[pl.ds(t + taps - 1 - k, STEP)]
                hid[at, :, lanes] = acc
                cross = acc * normed[at, :, lanes]
                sum_a[at] = sum_a[at] + acc * gain[None]
                sum_b[at] = sum_b[at] + cross * gain[None]
                return gain_sum + jnp.sum(cross, axis=0)

            zero = jnp.zeros((segs, LANES), F32)
            gacc[:, lanes] = gacc[:, lanes] + lax.fori_loop(0, frames // STEP, transposed, zero)

            def tap_sums(i, c):
                t = i * STEP
                g = gpad[pl.ds(t + half, STEP)]
                for k in range(taps):
                    kacc[k, :, lanes] = kacc[k, :, lanes] + jnp.sum(g * spad[pl.ds(t + k, STEP)], axis=0)
                return c

            lax.fori_loop(0, frames // STEP, tap_sums, 0)
            return carry

        lax.fori_loop(0, chunks, backward, 0)

        def sum_rows(b, carry):
            at = pl.ds(b * FB, FB)
            first = jnp.sum(sum_a[at], axis=2, keepdims=True)
            second = jnp.sum(sum_b[at], axis=2, keepdims=True)
            rows_a[b] = to_row(first, second, segs)
            return carry

        lax.fori_loop(0, blocks, sum_rows, 0)
        mom[2 * h + 1] = pack()
        copies = exchange(2 * h + 1)
        after()

        def prepare(b, carry):
            at = pl.ds(b * FB, FB)
            scale = scale_c[at][:, :, 0:1]
            grads = dy[pl.ds(b * (FB // 2), FB // 2)].astype(F32).reshape(FB, segs, width)
            hid[at] = grads + scale * (hid[at] * gain_ref[...].astype(F32)[None])
            normed[at] = scale * normed[at]
            return carry

        lax.fori_loop(0, blocks, prepare, 0)
        for copy in copies:
            copy.wait()
        row = sum(gathered(2 * h + 1)) * (1.0 / (shards * width))
        unpack(row, rows_a)
        unpack(pltpu.roll(row, LANES - segs, 1), rows_b)

        def finish(b, carry):
            at = pl.ds(b * FB, FB)
            plain = to_column(rows_a[b], segs)
            cross = to_column(rows_b[b], segs)
            scale = scale_c[at][:, :, 0:1]
            out = (hid[at] - scale * plain - normed[at] * cross).astype(BF16)
            out = out.reshape(FB // 2, 2, segs, width)
            for j in range(2):
                ret[h, j, pl.ds(b * (FB // 2), FB // 2)] = out[:, j]
            return carry

        lax.fori_loop(0, blocks, finish, 0)
        for j in range(2):
            scatter(ret.at[h, j], back.at[h, j], 7 + 2 * h + j)

    loads[2].wait()
    start_ring(0)
    go_on_ring(0)
    stage(0, lambda: start_ring(1), lambda: go_on_ring(1))
    stage(1, lambda: None, lambda: None)

    def weights():
        for k in range(taps):
            kgrad_ref[k] = jnp.sum(kacc[k], axis=0, keepdims=True)
        ggrad_ref[...] = jnp.sum(gacc[...], axis=0, keepdims=True)
        rows_of = frames * segs
        for j in range(shards):
            block = None
            for h in range(2):
                piece, d = pieces(h)[j]
                term = lax.dot_general(
                    hidden[h].reshape(rows_of, width), piece[...].reshape(rows_of, width),
                    (((0,), (0,)), ((), ())), preferred_element_type=F32,
                )
                block = term if block is None else block + term
            wgrad_ref[:, column(d)] = (block * grad_scale).astype(BF16)

    weights()
    sent(s0, r0, 1)
    for j in range(2):
        for h in range(2):
            arrived(ret.at[h, j], back.at[h, j], 7 + 2 * h + j)
        permute_home(j, home.at[j])
        scatter(home.at[j], home_ref.at[j], 11 + j)
    sent(langs_own, langs_all, 0)
    sent(s1, r1, 2)
    for h in range(2):
        sent(p_dy.at[h], own_dy.at[h], 3 + 2 * h)
        sent(p_x.at[h], own_x.at[h], 4 + 2 * h)
        for j in range(2):
            sent(ret.at[h, j], back.at[h, j], 7 + 2 * h + j)
        for copy in rings[h]:
            copy.wait_send()
    for j in range(2):
        arrived(home.at[j], home_ref.at[j], 11 + j)
        sent(home.at[j], home_ref.at[j], 11 + j)


def deliver_kernel(grad_scale, home_ref, w_ref, g_ref, k_ref, feat_ref, wgrad_ref, ggrad_ref, kgrad_ref):
    segs, frames, width = feat_ref.shape

    def join_frames(b, carry):
        at = pl.ds(b * (FB // 2), FB // 2)
        rows = jnp.stack([home_ref[0, at].astype(F32), home_ref[1, at].astype(F32)], axis=1)
        rows = rows.reshape(FB, segs, width)
        feat_ref[:, pl.ds(pl.multiple_of(b * FB, FB), FB), :] = jnp.swapaxes(rows, 0, 1).astype(BF16)
        return carry

    lax.fori_loop(0, frames // FB, join_frames, 0)
    wgrad_ref[...] = w_ref[...]
    ggrad_ref[...] = g_ref[...] * grad_scale
    kgrad_ref[...] = k_ref[...] * grad_scale


def per_device(feats, cotan, lang, w_out, gain, kernel):
    segs, frames, width = feats.shape
    owners = lax.axis_size("expert")
    shards = lax.axis_size("fsdp")
    taps = kernel.shape[1]
    total = owners * segs
    grad_scale = float(segs * frames) ** (-0.5)
    shape = jax.ShapeDtypeStruct
    half = segs // 2
    whole = pltpu.VMEM((owners, frames // owners, segs, width), BF16)
    halves = (owners, frames // owners, half, width)
    f32_rows = pltpu.VMEM((frames, half, width), F32)
    columns = pltpu.VMEM((frames, half, LANES), F32)
    padded = pltpu.VMEM((frames + 32, half, LANES), F32)
    rows = pltpu.VMEM((frames // FB, FB, LANES), F32)
    dma = pltpu.SemaphoreType.DMA
    vmem = pl.BlockSpec(memory_space=pltpu.VMEM)
    home, w_grad, gain_grad, tap_grad = pl.pallas_call(
        functools.partial(module_kernel, owners, shards, grad_scale),
        out_shape=(
            shape((2, owners, segs, width), BF16),
            shape(w_out.shape[1:], BF16),
            shape((1, width), F32),
            shape((taps, 1, width), F32),
        ),
        in_specs=[pl.BlockSpec(memory_space=pltpu.SMEM)] + [pl.BlockSpec(memory_space=pl.ANY)] * 3 + [vmem] * 2,
        out_specs=(vmem,) * 4,
        scratch_shapes=[
            pltpu.VMEM(feats.shape, BF16),
            pltpu.VMEM(feats.shape, BF16),
            pltpu.VMEM(w_out.shape[1:], BF16),
            pltpu.VMEM((2, owners, 1, LANES), F32),
            *[whole] * 4,
            *[pltpu.VMEM((2,) + halves, BF16)] * 4,
            pltpu.VMEM((2, shards - 1) + halves, BF16),
            pltpu.VMEM((2, 2, owners, half, width), BF16),
            pltpu.VMEM((2, 2, owners, half, width), BF16),
            pltpu.VMEM((2, owners, segs, width), BF16),
            pltpu.VMEM((total, total), BF16),
            pltpu.VMEM((total, total), BF16),
            f32_rows,
            f32_rows,
            pltpu.VMEM((2, frames, half, width), BF16),
            f32_rows,
            padded,
            padded,
            pltpu.VMEM((taps, half, width), F32),
            pltpu.VMEM((taps, half, width), F32),
            pltpu.VMEM((half, width), F32),
            columns,
            columns,
            columns,
            rows,
            rows,
            pltpu.VMEM((4, FB, LANES), F32),
            pltpu.VMEM((4, shards, FB, LANES), F32),
            dma((13,)),
            dma((13,)),
            dma((2, 6)),
            dma((2, 6)),
            dma((4, shards)),
            dma((4, shards)),
            dma((3,)),
        ],
        compiler_params=pltpu.CompilerParams(
            collective_id=0, has_side_effects=True, vmem_limit_bytes=67043328
        ),
        name="module_backward",
    )(lang, feats, cotan, w_out[0], gain, kernel[0])
    feat_grad, w_grad, gain_grad, tap_grad = pl.pallas_call(
        functools.partial(deliver_kernel, grad_scale),
        out_shape=(
            shape((segs, frames, width), BF16),
            shape(w_out.shape[1:], BF16),
            shape((1, width), F32),
            shape((taps, 1, width), F32),
        ),
        in_specs=[vmem] * 4,
        out_specs=(vmem,) * 4,
        name="deliver",
    )(home, w_grad, gain_grad, tap_grad)
    return feat_grad, w_grad[None], gain_grad, jnp.swapaxes(tap_grad, 0, 1)


def solution(mesh):
    in_specs = (
        P("expert", None, "fsdp"),
        P("expert", None, "fsdp"),
        P("expert"),
        P("expert", "fsdp", None),
        P("expert", "fsdp"),
        P("expert", None, "fsdp"),
    )
    out_specs = (
        P("expert", None, "fsdp"),
        P("expert", "fsdp", None),
        P("expert", "fsdp"),
        P("expert", None, "fsdp"),
    )
    return jax.shard_map(
        per_device, mesh=mesh, in_specs=in_specs, out_specs=out_specs, check_vma=False
    )
```

```python
import functools

import jax
import jax.numpy as jnp
from jax import lax
from jax.experimental import pallas as pl
from jax.experimental.pallas import tpu as pltpu
from jax.sharding import PartitionSpec as P

MESH = pl.DeviceIdType.MESH
F32 = jnp.float32
BF16 = jnp.bfloat16
LANES = 128
STEP = 16
FB = 16


def diagonal(segs):
    lane = lax.broadcasted_iota(jnp.int32, (1, segs, LANES), 2)
    seg = lax.broadcasted_iota(jnp.int32, (1, segs, LANES), 1)
    return lane == seg, lane == seg + segs


def to_row(first, second, segs):
    low, high = diagonal(segs)
    spread = jnp.where(low, first, 0.0) + jnp.where(high, second, 0.0)
    return jnp.sum(spread, axis=1)


def to_column(row, segs):
    low, _ = diagonal(segs)
    return jnp.sum(jnp.where(low, row[:, None, :], 0.0), axis=2, keepdims=True)


def mean_and_scale(rows, width, segs):
    n = len(rows)
    squares = [pltpu.roll(r, LANES - segs, 1) for r in rows]
    mean = sum(rows) * (1.0 / n)
    spread = sum((r - mean) * (r - mean) for r in rows)
    var = (sum(squares) + width * spread) * (1.0 / (n * width))
    return mean, lax.rsqrt(var + 1e-05)


def module_kernel(
    owners, shards, grad_scale,
    lang_ref, x_ref, dy_ref, w_ref, gain_ref, taps_ref,
    home_ref, wgrad_ref, ggrad_ref, kgrad_ref,
    x_vmem, dy_vmem, w_vmem, langs, s0, s1, r0, r1, p_dy, p_x, own_dy, own_x, ring, ret, back, home, pick, pick_t,
    normed, slope, hidden, hid, gpad, spad, tapb, kacc, gacc, sum_a, sum_b, scale_c, rows_a, rows_b, mom, parts,
    send, recv, ring_send, ring_recv, ex_send, ex_recv, load,
):
    all_segs, frames, width = x_ref.shape
    segs = own_x.shape[3]
    taps = taps_ref.shape[0]
    half = taps // 2
    total = owners * all_segs
    part = owners * segs
    chunks = width // LANES
    blocks = frames // FB
    me = lax.axis_index("expert")
    fs = lax.axis_index("fsdp")
    peer_x = [lax.rem(fs + d, shards) for d in range(shards)]

    barrier = pltpu.get_barrier_semaphore()

    def greet(d, carry):
        pl.semaphore_signal(
            barrier, inc=1, device_id={"expert": lax.rem(me + d, owners)}, device_id_type=MESH
        )
        return carry

    loads = [
        pltpu.make_async_copy(src, dst, load.at[i])
        for i, (src, dst) in enumerate(((dy_ref, dy_vmem), (x_ref, x_vmem), (w_ref, w_vmem)))
    ]
    for copy in loads:
        copy.start()
    lax.fori_loop(1, owners, greet, 0)
    for d in range(1, shards):
        pl.semaphore_signal(barrier, inc=1, device_id={"fsdp": peer_x[d]}, device_id_type=MESH)

    def split_frames(src, dst):
        def block(b, carry):
            rows = src[:, pl.ds(pl.multiple_of(b * FB, FB), FB), :].astype(F32)
            moved = jnp.swapaxes(rows, 0, 1).astype(BF16)
            dst[pl.ds(b * (FB // 2), FB // 2)] = moved.reshape(FB // 2, 2, all_segs, width)
            return carry

        lax.fori_loop(0, blocks, block, 0)

    def scatter(src, dst, i):
        def one(p):
            pltpu.make_async_remote_copy(
                src_ref=src.at[p], dst_ref=dst.at[me], send_sem=send.at[i], recv_sem=recv.at[i],
                device_id={"expert": p}, device_id_type=MESH,
            ).start()

        def both(d, carry):
            one(lax.rem(me + d, owners))
            one(lax.rem(me + owners - d, owners))
            return carry

        lax.fori_loop(1, owners // 2, both, 0)
        one(lax.rem(me + owners // 2, owners))
        pltpu.make_async_copy(src.at[me], dst.at[me], recv.at[i]).start()

    def arrived(src, dst, i):
        pltpu.make_async_copy(src, dst, recv.at[i]).wait()

    def sent(src, dst, i):
        most = pl.ds(0, owners - 1)
        pltpu.make_async_remote_copy(
            src_ref=src.at[most], dst_ref=dst.at[most], send_sem=send.at[i], recv_sem=recv.at[i],
            device_id={"expert": lax.rem(me + 1, owners)}, device_id_type=MESH,
        ).wait_send()

    lane = lax.broadcasted_iota(jnp.int32, (1, LANES), 1)
    first_lane = lax.rem(me, LANES // all_segs) * all_segs
    lang_row = jnp.zeros((1, LANES), jnp.int32)
    for i in range(all_segs):
        lang_row = jnp.where(lane == first_lane + i, lang_ref[i], lang_row)
    lang_row = lang_row.astype(F32)
    loads[0].wait()
    split_frames(dy_vmem, s0)
    langs_own = langs.at[0]
    langs_all = langs.at[1]

    def spread_langs(d, carry):
        langs_own[d] = lang_row
        return carry

    lax.fori_loop(0, owners, spread_langs, 0)
    pl.semaphore_wait(barrier, owners - 1 + shards - 1)
    scatter(langs_own, langs_all, 0)
    scatter(s0, r0, 1)
    loads[1].wait()
    split_frames(x_vmem, s1)
    scatter(s1, r1, 2)

    for k in range(taps):
        tapb[k] = jnp.broadcast_to(taps_ref[k : k + 1, :].astype(F32), (segs, width))
    for pad in (gpad, spad):
        for h in range(2):
            for c in range(chunks):
                pad[h, c, :half] = jnp.zeros((half, segs, LANES), F32)
                pad[h, c, half + frames :] = jnp.zeros((pad.shape[2] - half - frames, segs, LANES), F32)
    kacc[...] = jnp.zeros_like(kacc)
    gacc[...] = jnp.zeros_like(gacc)

    arrived(langs_own, langs_all, 0)
    owner_of = lax.broadcasted_iota(jnp.int32, (owners, LANES), 0).astype(F32)
    before = lax.broadcasted_iota(jnp.int32, (LANES, LANES), 0) < lax.broadcasted_iota(
        jnp.int32, (LANES, LANES), 1
    )
    before = jnp.where(before, 1.0, 0.0).astype(BF16)
    place = lax.broadcasted_iota(jnp.int32, (total, LANES), 0).astype(F32)
    base = jnp.zeros((owners, 1), F32)
    group = LANES // all_segs
    for q in range(total // LANES):
        row = jnp.sum(langs_all[q * group : (q + 1) * group], axis=0)
        match = jnp.where(owner_of == row, 1.0, 0.0)
        rank = jnp.dot(match.astype(BF16), before, preferred_element_type=F32) + base
        base = base + jnp.sum(match, axis=1, keepdims=True)
        spot = owner_of * segs + rank + jnp.where(rank >= segs, float(part - segs), 0.0)
        dest = jnp.sum(match * spot, axis=0, keepdims=True)
        pick[:, q * LANES : (q + 1) * LANES] = jnp.where(place == dest, 1.0, 0.0).astype(BF16)
    number = lax.broadcasted_iota(jnp.int32, (16, total), 1)
    which = lax.broadcasted_iota(jnp.int32, (16, total), 0)
    digits = jnp.where(which == 0, number // 32, number % 32).astype(F32).astype(BF16)
    found = lax.dot_general(digits, pick[...], (((1,), (1,)), ((), ())), preferred_element_type=F32)
    source = found[0:1] * 32.0 + found[1:2]
    for q in range(total // LANES):
        cols = slice(q * LANES, (q + 1) * LANES)
        pick_t[:, cols] = jnp.where(place == source[:, cols], 1.0, 0.0).astype(BF16)

    def permute_out(h, src, dst):
        rows = 256

        def block(b, carry):
            choice = pick[pl.ds(pl.multiple_of(h * part + b * rows, rows), rows), :]
            for j in range(2):
                flat = src[:, j].reshape(total, width)
                moved = jnp.dot(choice, flat, preferred_element_type=F32).astype(BF16)
                dst[pl.ds(b * (rows // segs), rows // segs), j] = moved.reshape(rows // segs, segs, width)
            return carry

        lax.fori_loop(0, part // rows, block, 0)

    def permute_home(j, dst):
        rows = 256

        def block(b, carry):
            at = pl.ds(pl.multiple_of(b * rows, rows), rows)
            moved = None
            for h in range(2):
                flat = back[h, j].reshape(part, width)
                term = jnp.dot(pick_t[at, h * part : (h + 1) * part], flat, preferred_element_type=F32)
                moved = term if moved is None else moved + term
            moved = moved.astype(BF16).reshape(rows // all_segs, all_segs, width)
            dst[pl.ds(b * (rows // all_segs), rows // all_segs)] = moved
            return carry

        lax.fori_loop(0, total // rows, block, 0)

    arrived(s0, r0, 1)
    permute_out(0, r0, p_dy.at[0])
    scatter(p_dy.at[0], own_dy.at[0], 3)
    permute_out(1, r0, p_dy.at[1])
    arrived(s1, r1, 2)
    permute_out(0, r1, p_x.at[0])
    scatter(p_x.at[0], own_x.at[0], 4)
    scatter(p_dy.at[1], own_dy.at[1], 5)
    permute_out(1, r1, p_x.at[1])
    scatter(p_x.at[1], own_x.at[1], 6)

    def ring_copy(h, src, dst, i, d):
        return pltpu.make_async_remote_copy(
            src_ref=src, dst_ref=dst, send_sem=ring_send.at[h, i], recv_sem=ring_recv.at[h, i],
            device_id={"fsdp": peer_x[d]}, device_id_type=MESH,
        )

    middle = owners // 2

    def ring_copies(h):
        own = own_dy.at[h]
        one = ring.at[h, 0]
        two = ring.at[h, 1]
        far = ring.at[h, 2]
        low = pl.ds(0, middle)
        high = pl.ds(middle, middle)
        return [
            ring_copy(h, own.at[low], one.at[low], 0, 1),
            ring_copy(h, own.at[high], two.at[high], 1, shards - 1),
            ring_copy(h, own.at[high], one.at[high], 2, 1),
            ring_copy(h, own.at[low], two.at[low], 3, shards - 1),
            ring_copy(h, one.at[low], far.at[low], 4, 1),
            ring_copy(h, two.at[high], far.at[high], 5, shards - 1),
        ]

    rings = [ring_copies(0), ring_copies(1)]

    def start_ring(h):
        arrived(p_dy.at[h], own_dy.at[h], 3 + 2 * h)
        rings[h][0].start()
        rings[h][1].start()

    def go_on_ring(h):
        rings[h][2].start()
        rings[h][3].start()

    def exchange(i):
        copies = [
            pltpu.make_async_remote_copy(
                src_ref=mom.at[i], dst_ref=parts.at[i, d], send_sem=ex_send.at[i, d],
                recv_sem=ex_recv.at[i, d], device_id={"fsdp": peer_x[d]}, device_id_type=MESH,
            )
            for d in range(1, shards)
        ]
        for copy in copies:
            copy.start()
        return copies

    def gathered(i):
        return [mom[i]] + [parts[i, d] for d in range(1, shards)]

    def pack():
        packed = rows_a[0]
        for b in range(1, blocks):
            packed = packed + pltpu.roll(rows_a[b], 2 * segs * b, 1)
        return packed

    def unpack(packed, dst):
        dst[0] = packed
        for b in range(1, blocks):
            dst[b] = pltpu.roll(packed, LANES - 2 * segs * b, 1)

    def column(d):
        return pl.ds(pl.multiple_of(peer_x[d] * width, LANES), width)

    def pieces(h):
        return [
            (own_dy.at[h], 0), (ring.at[h, 0], shards - 1), (ring.at[h, 1], 1), (ring.at[h, 2], 2)
        ]

    def stage(h, between, after):
        dy = own_dy.at[h]
        x_own = own_x.at[h]
        arrived(p_x.at[h], x_own, 4 + 2 * h)

        def moments(b, carry):
            x = x_own[pl.ds(b * (FB // 2), FB // 2)].astype(F32).reshape(FB, segs, width)
            mean = jnp.sum(x, axis=2, keepdims=True) * (1.0 / width)
            centre = x - mean
            square = jnp.sum(centre * centre, axis=2, keepdims=True)
            rows_a[b] = to_row(mean, square, segs)
            return carry

        lax.fori_loop(0, blocks, moments, 0)
        mom[2 * h] = pack()
        copies = exchange(2 * h)
        for copy in rings[h][:4]:
            copy.wait_recv()
        rings[h][4].start()
        rings[h][5].start()

        def hid_rows(b, chosen):
            acc = None
            for piece, d in chosen:
                rows = piece[pl.ds(b * FB, FB)].reshape(2 * FB * segs, width)
                term = lax.dot_general(
                    rows, w_vmem[:, column(d)], (((1,), (1,)), ((), ())), preferred_element_type=F32
                )
                acc = term if acc is None else acc + term
            return acc.reshape(2 * FB, segs, width)

        def hid_near(b, carry):
            hid[pl.ds(b * 2 * FB, 2 * FB)] = hid_rows(b, pieces(h)[:3])
            return carry

        def hid_far(b, carry):
            at = pl.ds(b * 2 * FB, 2 * FB)
            hid[at] = hid[at] + hid_rows(b, pieces(h)[3:])
            return carry

        lax.fori_loop(0, blocks // 2, hid_near, 0)
        for copy in copies:
            copy.wait()
        mean_row, scale_row = mean_and_scale(gathered(2 * h), width, segs)
        unpack(mean_row, rows_a)
        unpack(scale_row, rows_b)

        def normalize(b, carry):
            at = pl.ds(b * FB, FB)
            mean = to_column(rows_a[b], segs)
            scale = to_column(rows_b[b], segs)
            x = x_own[pl.ds(b * (FB // 2), FB // 2)].astype(F32).reshape(FB, segs, width)
            normed[at] = (x - mean) * scale
            scale_c[at] = jnp.broadcast_to(scale, (FB, segs, LANES))
            return carry

        lax.fori_loop(0, blocks, normalize, 0)

        def convolve(lb, carry):
            lanes = pl.ds(pl.multiple_of(lb * LANES, LANES), LANES)
            gain = gain_ref[:, lanes].astype(F32)

            def fill(i, c):
                at = pl.ds(i * FB, FB)
                spad[h, lb, pl.ds(i * FB + half, FB)] = normed[at, :, lanes] * gain[None]
                return c

            lax.fori_loop(0, blocks, fill, 0)

            def step(i, c):
                t = i * STEP
                acc = tapb[0, :, lanes][None] * spad[h, lb, pl.ds(t, STEP)]
                for k in range(1, taps):
                    acc = acc + tapb[k, :, lanes][None] * spad[h, lb, pl.ds(t + k, STEP)]
                gate = 1.0 / (1.0 + jnp.exp(-acc))
                out = acc * gate
                slope[pl.ds(t, STEP), :, lanes] = gate + out * (1.0 - gate)
                hidden[h, pl.ds(t, STEP), :, lanes] = out.astype(BF16)
                return c

            lax.fori_loop(0, frames // STEP, step, 0)
            return carry

        lax.fori_loop(0, chunks, convolve, 0)
        rings[h][4].wait_recv()
        rings[h][5].wait_recv()
        lax.fori_loop(0, blocks // 2, hid_far, 0)
        between()
        sum_a[...] = jnp.zeros_like(sum_a)
        sum_b[...] = jnp.zeros_like(sum_b)

        def backward(lb, carry):
            lanes = pl.ds(pl.multiple_of(lb * LANES, LANES), LANES)
            gain = gain_ref[:, lanes].astype(F32)

            def fill(i, c):
                at = pl.ds(i * STEP, STEP)
                gpad[h, lb, pl.ds(i * STEP + half, STEP)] = hid[at, :, lanes] * slope[at, :, lanes]
                return c

            lax.fori_loop(0, frames // STEP, fill, 0)

            def transposed(i, gain_sum):
                t = i * STEP
                at = pl.ds(t, STEP)
                acc = tapb[0, :, lanes][None] * gpad[h, lb, pl.ds(t + taps - 1, STEP)]
                for k in range(1, taps):
                    acc = acc + tapb[k, :, lanes][None] * gpad[h, lb, pl.ds(t + taps - 1 - k, STEP)]
                hid[at, :, lanes] = acc
                cross = acc * normed[at, :, lanes]
                sum_a[at] = sum_a[at] + acc * gain[None]
                sum_b[at] = sum_b[at] + cross * gain[None]
                return gain_sum + jnp.sum(cross, axis=0)

            zero = jnp.zeros((segs, LANES), F32)
            gacc[:, lanes] = gacc[:, lanes] + lax.fori_loop(0, frames // STEP, transposed, zero)

            return carry

        lax.fori_loop(0, chunks, backward, 0)

        def sum_rows(b, carry):
            at = pl.ds(b * FB, FB)
            first = jnp.sum(sum_a[at], axis=2, keepdims=True)
            second = jnp.sum(sum_b[at], axis=2, keepdims=True)
            rows_a[b] = to_row(first, second, segs)
            return carry

        lax.fori_loop(0, blocks, sum_rows, 0)
        mom[2 * h + 1] = pack()
        copies = exchange(2 * h + 1)
        after()

        def prepare(b, carry):
            at = pl.ds(b * FB, FB)
            scale = scale_c[at][:, :, 0:1]
            grads = dy[pl.ds(b * (FB // 2), FB // 2)].astype(F32).reshape(FB, segs, width)
            hid[at] = grads + scale * (hid[at] * gain_ref[...].astype(F32)[None])
            normed[at] = scale * normed[at]
            return carry

        lax.fori_loop(0, blocks, prepare, 0)
        for copy in copies:
            copy.wait()
        row = sum(gathered(2 * h + 1)) * (1.0 / (shards * width))
        unpack(row, rows_a)
        unpack(pltpu.roll(row, LANES - segs, 1), rows_b)

        def finish(b, carry):
            at = pl.ds(b * FB, FB)
            plain = to_column(rows_a[b], segs)
            cross = to_column(rows_b[b], segs)
            scale = scale_c[at][:, :, 0:1]
            out = (hid[at] - scale * plain - normed[at] * cross).astype(BF16)
            out = out.reshape(FB // 2, 2, segs, width)
            for j in range(2):
                ret[h, j, pl.ds(b * (FB // 2), FB // 2)] = out[:, j]
            return carry

        lax.fori_loop(0, blocks, finish, 0)
        for j in range(2):
            scatter(ret.at[h, j], back.at[h, j], 7 + 2 * h + j)

    loads[2].wait()
    start_ring(0)
    go_on_ring(0)
    stage(0, lambda: start_ring(1), lambda: go_on_ring(1))
    stage(1, lambda: None, lambda: None)

    def tap_grads(lb, carry):
        lanes = pl.ds(pl.multiple_of(lb * LANES, LANES), LANES)
        for h in range(2):

            def tap_sums(i, c):
                t = i * STEP
                g = gpad[h, lb, pl.ds(t + half, STEP)]
                for k in range(taps):
                    term = jnp.sum(g * spad[h, lb, pl.ds(t + k, STEP)], axis=0)
                    kacc[k, :, lanes] = kacc[k, :, lanes] + term
                return c

            lax.fori_loop(0, frames // STEP, tap_sums, 0)
        return carry

    def weights():
        lax.fori_loop(0, chunks, tap_grads, 0)
        for k in range(taps):
            kgrad_ref[k] = jnp.sum(kacc[k], axis=0, keepdims=True)
        ggrad_ref[...] = jnp.sum(gacc[...], axis=0, keepdims=True)
        rows_of = frames * segs
        for j in range(shards):
            block = None
            for h in range(2):
                piece, d = pieces(h)[j]
                term = lax.dot_general(
                    hidden[h].reshape(rows_of, width), piece[...].reshape(rows_of, width),
                    (((0,), (0,)), ((), ())), preferred_element_type=F32,
                )
                block = term if block is None else block + term
            wgrad_ref[:, column(d)] = (block * grad_scale).astype(BF16)

    weights()
    sent(s0, r0, 1)
    for j in range(2):
        for h in range(2):
            arrived(ret.at[h, j], back.at[h, j], 7 + 2 * h + j)
        permute_home(j, home.at[j])
        scatter(home.at[j], home_ref.at[j], 11 + j)
    sent(langs_own, langs_all, 0)
    sent(s1, r1, 2)
    for h in range(2):
        sent(p_dy.at[h], own_dy.at[h], 3 + 2 * h)
        sent(p_x.at[h], own_x.at[h], 4 + 2 * h)
        for j in range(2):
            sent(ret.at[h, j], back.at[h, j], 7 + 2 * h + j)
        for copy in rings[h]:
            copy.wait_send()
    for j in range(2):
        arrived(home.at[j], home_ref.at[j], 11 + j)
        sent(home.at[j], home_ref.at[j], 11 + j)


def deliver_kernel(grad_scale, home_ref, w_ref, g_ref, k_ref, feat_ref, wgrad_ref, ggrad_ref, kgrad_ref):
    segs, frames, width = feat_ref.shape

    def join_frames(b, carry):
        at = pl.ds(b * (FB // 2), FB // 2)
        rows = jnp.stack([home_ref[0, at].astype(F32), home_ref[1, at].astype(F32)], axis=1)
        rows = rows.reshape(FB, segs, width)
        feat_ref[:, pl.ds(pl.multiple_of(b * FB, FB), FB), :] = jnp.swapaxes(rows, 0, 1).astype(BF16)
        return carry

    lax.fori_loop(0, frames // FB, join_frames, 0)
    wgrad_ref[...] = w_ref[...]
    ggrad_ref[...] = g_ref[...] * grad_scale
    kgrad_ref[...] = k_ref[...] * grad_scale


def per_device(feats, cotan, lang, w_out, gain, kernel):
    segs, frames, width = feats.shape
    owners = lax.axis_size("expert")
    shards = lax.axis_size("fsdp")
    taps = kernel.shape[1]
    total = owners * segs
    grad_scale = float(segs * frames) ** (-0.5)
    shape = jax.ShapeDtypeStruct
    half = segs // 2
    whole = pltpu.VMEM((owners, frames // owners, segs, width), BF16)
    halves = (owners, frames // owners, half, width)
    f32_rows = pltpu.VMEM((frames, half, width), F32)
    columns = pltpu.VMEM((frames, half, LANES), F32)
    padded = pltpu.VMEM((2, width // LANES, frames + 32, half, LANES), F32)
    rows = pltpu.VMEM((frames // FB, FB, LANES), F32)
    dma = pltpu.SemaphoreType.DMA
    vmem = pl.BlockSpec(memory_space=pltpu.VMEM)
    home, w_grad, gain_grad, tap_grad = pl.pallas_call(
        functools.partial(module_kernel, owners, shards, grad_scale),
        out_shape=(
            shape((2, owners, segs, width), BF16),
            shape(w_out.shape[1:], BF16),
            shape((1, width), F32),
            shape((taps, 1, width), F32),
        ),
        in_specs=[pl.BlockSpec(memory_space=pltpu.SMEM)] + [pl.BlockSpec(memory_space=pl.ANY)] * 3 + [vmem] * 2,
        out_specs=(vmem,) * 4,
        scratch_shapes=[
            pltpu.VMEM(feats.shape, BF16),
            pltpu.VMEM(feats.shape, BF16),
            pltpu.VMEM(w_out.shape[1:], BF16),
            pltpu.VMEM((2, owners, 1, LANES), F32),
            *[whole] * 4,
            *[pltpu.VMEM((2,) + halves, BF16)] * 4,
            pltpu.VMEM((2, shards - 1) + halves, BF16),
            pltpu.VMEM((2, 2, owners, half, width), BF16),
            pltpu.VMEM((2, 2, owners, half, width), BF16),
            pltpu.VMEM((2, owners, segs, width), BF16),
            pltpu.VMEM((total, total), BF16),
            pltpu.VMEM((total, total), BF16),
            f32_rows,
            f32_rows,
            pltpu.VMEM((2, frames, half, width), BF16),
            f32_rows,
            padded,
            padded,
            pltpu.VMEM((taps, half, width), F32),
            pltpu.VMEM((taps, half, width), F32),
            pltpu.VMEM((half, width), F32),
            columns,
            columns,
            columns,
            rows,
            rows,
            pltpu.VMEM((4, FB, LANES), F32),
            pltpu.VMEM((4, shards, FB, LANES), F32),
            dma((13,)),
            dma((13,)),
            dma((2, 6)),
            dma((2, 6)),
            dma((4, shards)),
            dma((4, shards)),
            dma((3,)),
        ],
        compiler_params=pltpu.CompilerParams(
            collective_id=0, has_side_effects=True, vmem_limit_bytes=67043328
        ),
        name="module_backward",
    )(lang, feats, cotan, w_out[0], gain, kernel[0])
    feat_grad, w_grad, gain_grad, tap_grad = pl.pallas_call(
        functools.partial(deliver_kernel, grad_scale),
        out_shape=(
            shape((segs, frames, width), BF16),
            shape(w_out.shape[1:], BF16),
            shape((1, width), F32),
            shape((taps, 1, width), F32),
        ),
        in_specs=[vmem] * 4,
        out_specs=(vmem,) * 4,
        name="deliver",
    )(home, w_grad, gain_grad, tap_grad)
    return feat_grad, w_grad[None], gain_grad, jnp.swapaxes(tap_grad, 0, 1)


def solution(mesh):
    in_specs = (
        P("expert", None, "fsdp"),
        P("expert", None, "fsdp"),
        P("expert"),
        P("expert", "fsdp", None),
        P("expert", "fsdp"),
        P("expert", None, "fsdp"),
    )
    out_specs = (
        P("expert", None, "fsdp"),
        P("expert", "fsdp", None),
        P("expert", "fsdp"),
        P("expert", None, "fsdp"),
    )
    return jax.shard_map(
        per_device, mesh=mesh, in_specs=in_specs, out_specs=out_specs, check_vma=False
    )
```

```python
import functools

import jax
import jax.numpy as jnp
from jax import lax
from jax.experimental import pallas as pl
from jax.experimental.pallas import tpu as pltpu
from jax.sharding import PartitionSpec as P

MESH = pl.DeviceIdType.MESH
F32 = jnp.float32
BF16 = jnp.bfloat16
LANES = 128
STEP = 16
FB = 16


def diagonal(segs):
    lane = lax.broadcasted_iota(jnp.int32, (1, segs, LANES), 2)
    seg = lax.broadcasted_iota(jnp.int32, (1, segs, LANES), 1)
    return lane == seg, lane == seg + segs


def to_row(first, second, segs):
    low, high = diagonal(segs)
    spread = jnp.where(low, first, 0.0) + jnp.where(high, second, 0.0)
    return jnp.sum(spread, axis=1)


def to_column(row, segs):
    low, _ = diagonal(segs)
    return jnp.sum(jnp.where(low, row[:, None, :], 0.0), axis=2, keepdims=True)


def mean_and_scale(rows, width, segs):
    n = len(rows)
    squares = [pltpu.roll(r, LANES - segs, 1) for r in rows]
    mean = sum(rows) * (1.0 / n)
    spread = sum((r - mean) * (r - mean) for r in rows)
    var = (sum(squares) + width * spread) * (1.0 / (n * width))
    return mean, lax.rsqrt(var + 1e-05)


def module_kernel(
    owners, shards, grad_scale,
    lang_ref, x_ref, dy_ref, w_ref, gain_ref, taps_ref,
    home_ref, wgrad_ref, ggrad_ref, kgrad_ref,
    x_vmem, dy_vmem, w_vmem, langs, s0, s1, r0, r1, p_dy, p_x, own_dy, own_x, ring, ret, back, home, pick, pick_t,
    normed, slope, hidden, hid, gpad, spad, tapb, kacc, gacc, sum_a, sum_b, scale_c, rows_a, rows_b, mom, parts,
    send, recv, ring_send, ring_recv, ex_send, ex_recv, load, w_block,
):
    all_segs, frames, width = x_ref.shape
    segs = own_x.shape[3]
    taps = taps_ref.shape[0]
    half = taps // 2
    total = owners * all_segs
    part = owners * segs
    chunks = width // LANES
    blocks = frames // FB
    me = lax.axis_index("expert")
    fs = lax.axis_index("fsdp")
    peer_x = [lax.rem(fs + d, shards) for d in range(shards)]

    barrier = pltpu.get_barrier_semaphore()

    def greet(d, carry):
        pl.semaphore_signal(
            barrier, inc=1, device_id={"expert": lax.rem(me + d, owners)}, device_id_type=MESH
        )
        return carry

    loads = [
        pltpu.make_async_copy(src, dst, load.at[i])
        for i, (src, dst) in enumerate(((dy_ref, dy_vmem), (x_ref, x_vmem), (w_ref, w_vmem)))
    ]
    for copy in loads:
        copy.start()
    lax.fori_loop(1, owners, greet, 0)
    for d in range(1, shards):
        pl.semaphore_signal(barrier, inc=1, device_id={"fsdp": peer_x[d]}, device_id_type=MESH)

    def split_frames(src, dst):
        def block(b, carry):
            rows = src[:, pl.ds(pl.multiple_of(b * FB, FB), FB), :].astype(F32)
            moved = jnp.swapaxes(rows, 0, 1).astype(BF16)
            dst[pl.ds(b * (FB // 2), FB // 2)] = moved.reshape(FB // 2, 2, all_segs, width)
            return carry

        lax.fori_loop(0, blocks, block, 0)

    def pair_of(p):
        return lax.rem(p, 2) * (owners // 2) + lax.div(p, 2)

    def same(p):
        return p

    def send_block(src, dst, i, p, src_at, dst_at):
        pltpu.make_async_remote_copy(
            src_ref=src.at[src_at(p)], dst_ref=dst.at[dst_at(me)], send_sem=send.at[i], recv_sem=recv.at[i],
            device_id={"expert": p}, device_id_type=MESH,
        ).start()

    def keep_block(src, dst, i, src_at, dst_at):
        pltpu.make_async_copy(src.at[src_at(me)], dst.at[dst_at(me)], recv.at[i]).start()

    def scatter(src, dst, i, src_at, dst_at):
        def both(d, carry):
            send_block(src, dst, i, lax.rem(me + d, owners), src_at, dst_at)
            send_block(src, dst, i, lax.rem(me + owners - d, owners), src_at, dst_at)
            return carry

        lax.fori_loop(1, owners // 2, both, 0)
        send_block(src, dst, i, lax.rem(me + owners // 2, owners), src_at, dst_at)
        keep_block(src, dst, i, src_at, dst_at)

    def scatter_half(src, dst, i, c):
        count = owners // 2
        mine = lax.div(me, 2)

        def one(d, carry):
            send_block(src, dst, i, lax.rem(mine + d, count) * 2 + c, pair_of, same)
            return carry

        lax.fori_loop(1, count, one, 0)

        @pl.when(lax.rem(me, 2) == c)
        def _():
            keep_block(src, dst, i, pair_of, same)

        @pl.when(lax.rem(me, 2) != c)
        def _():
            send_block(src, dst, i, mine * 2 + c, pair_of, same)

    def arrived(src, dst, i):
        pltpu.make_async_copy(src, dst, recv.at[i]).wait()

    def sent(src, dst, i):
        most = pl.ds(0, owners - 1)
        pltpu.make_async_remote_copy(
            src_ref=src.at[most], dst_ref=dst.at[most], send_sem=send.at[i], recv_sem=recv.at[i],
            device_id={"expert": lax.rem(me + 1, owners)}, device_id_type=MESH,
        ).wait_send()

    lane = lax.broadcasted_iota(jnp.int32, (1, LANES), 1)
    first_lane = lax.rem(me, LANES // all_segs) * all_segs
    lang_row = jnp.zeros((1, LANES), jnp.int32)
    for i in range(all_segs):
        lang_row = jnp.where(lane == first_lane + i, lang_ref[i], lang_row)
    lang_row = lang_row.astype(F32)
    loads[0].wait()
    split_frames(dy_vmem, s0)
    langs_own = langs.at[0]
    langs_all = langs.at[1]

    def spread_langs(d, carry):
        langs_own[d] = lang_row
        return carry

    lax.fori_loop(0, owners, spread_langs, 0)
    pl.semaphore_wait(barrier, owners - 1 + shards - 1)
    scatter(langs_own, langs_all, 0, same, same)
    scatter(s0, r0, 1, pair_of, same)
    loads[1].wait()
    split_frames(x_vmem, s1)
    scatter(s1, r1, 2, pair_of, same)

    for k in range(taps):
        tapb[k] = jnp.broadcast_to(taps_ref[k : k + 1, :].astype(F32), (segs, width))
    for pad in (gpad, spad):
        for h in range(2):
            for c in range(chunks):
                pad[h, c, :half] = jnp.zeros((half, segs, LANES), F32)
                pad[h, c, half + frames :] = jnp.zeros((pad.shape[2] - half - frames, segs, LANES), F32)
    kacc[...] = jnp.zeros_like(kacc)
    gacc[...] = jnp.zeros_like(gacc)

    arrived(langs_own, langs_all, 0)
    owner_of = lax.broadcasted_iota(jnp.int32, (owners, LANES), 0).astype(F32)
    before = lax.broadcasted_iota(jnp.int32, (LANES, LANES), 0) < lax.broadcasted_iota(
        jnp.int32, (LANES, LANES), 1
    )
    before = jnp.where(before, 1.0, 0.0).astype(BF16)
    place = lax.broadcasted_iota(jnp.int32, (total, LANES), 0).astype(F32)
    base = jnp.zeros((owners, 1), F32)
    group = LANES // all_segs
    for q in range(total // LANES):
        row = jnp.sum(langs_all[q * group : (q + 1) * group], axis=0)
        match = jnp.where(owner_of == row, 1.0, 0.0)
        rank = jnp.dot(match.astype(BF16), before, preferred_element_type=F32) + base
        base = base + jnp.sum(match, axis=1, keepdims=True)
        spot = owner_of * segs + rank + jnp.where(rank >= segs, float(part - segs), 0.0)
        dest = jnp.sum(match * spot, axis=0, keepdims=True)
        pick[:, q * LANES : (q + 1) * LANES] = jnp.where(place == dest, 1.0, 0.0).astype(BF16)
    number = lax.broadcasted_iota(jnp.int32, (16, total), 1)
    which = lax.broadcasted_iota(jnp.int32, (16, total), 0)
    digits = jnp.where(which == 0, number // 32, number % 32).astype(F32).astype(BF16)
    found = lax.dot_general(digits, pick[...], (((1,), (1,)), ((), ())), preferred_element_type=F32)
    source = found[0:1] * 32.0 + found[1:2]
    for q in range(total // LANES):
        cols = slice(q * LANES, (q + 1) * LANES)
        pick_t[:, cols] = jnp.where(place == source[:, cols], 1.0, 0.0).astype(BF16)

    def permute_out(h, src, dst):
        rows = 256

        def block(b, carry):
            choice = pick[pl.ds(pl.multiple_of(h * part + b * rows, rows), rows), :]
            for j in range(2):
                flat = src[:, j].reshape(total, width)
                moved = jnp.dot(choice, flat, preferred_element_type=F32).astype(BF16)
                dst[pl.ds(b * (rows // segs), rows // segs), j] = moved.reshape(rows // segs, segs, width)
            return carry

        lax.fori_loop(0, part // rows, block, 0)

    def permute_home(j, dst):
        rows = 256

        def block(b, carry):
            at = pl.ds(pl.multiple_of(b * rows, rows), rows)
            moved = None
            for h in range(2):
                flat = back[h, j].reshape(part, width)
                term = jnp.dot(pick_t[at, h * part : (h + 1) * part], flat, preferred_element_type=F32)
                moved = term if moved is None else moved + term
            moved = moved.astype(BF16).reshape(rows // all_segs, all_segs, width)
            dst[pl.ds(b * (rows // all_segs), rows // all_segs)] = moved
            return carry

        lax.fori_loop(0, total // rows, block, 0)

    arrived(s0, r0, 1)
    permute_out(0, r0, p_dy.at[0])
    scatter(p_dy.at[0], own_dy.at[0], 3, same, pair_of)
    permute_out(1, r0, p_dy.at[1])
    arrived(s1, r1, 2)
    permute_out(0, r1, p_x.at[0])
    scatter(p_x.at[0], own_x.at[0], 4, same, pair_of)
    scatter(p_dy.at[1], own_dy.at[1], 5, same, pair_of)
    permute_out(1, r1, p_x.at[1])
    scatter(p_x.at[1], own_x.at[1], 6, same, pair_of)

    def ring_copy(h, src, dst, i, d):
        return pltpu.make_async_remote_copy(
            src_ref=src, dst_ref=dst, send_sem=ring_send.at[h, i], recv_sem=ring_recv.at[h, i],
            device_id={"fsdp": peer_x[d]}, device_id_type=MESH,
        )

    middle = owners // 2

    def ring_copies(h):
        own = own_dy.at[h]
        one = ring.at[h, 0]
        two = ring.at[h, 1]
        far = ring.at[h, 2]
        low = pl.ds(0, middle)
        high = pl.ds(middle, middle)
        return [
            ring_copy(h, own.at[low], one.at[low], 0, 1),
            ring_copy(h, own.at[high], two.at[high], 1, shards - 1),
            ring_copy(h, own.at[high], one.at[high], 2, 1),
            ring_copy(h, own.at[low], two.at[low], 3, shards - 1),
            ring_copy(h, one.at[low], far.at[low], 4, 1),
            ring_copy(h, two.at[high], far.at[high], 5, shards - 1),
        ]

    rings = [ring_copies(0), ring_copies(1)]

    def start_ring(h):
        arrived(p_dy.at[h], own_dy.at[h], 3 + 2 * h)
        rings[h][0].start()
        rings[h][1].start()

    def go_on_ring(h):
        rings[h][2].start()
        rings[h][3].start()

    def exchange(i):
        copies = [
            pltpu.make_async_remote_copy(
                src_ref=mom.at[i], dst_ref=parts.at[i, d], send_sem=ex_send.at[i, d],
                recv_sem=ex_recv.at[i, d], device_id={"fsdp": peer_x[d]}, device_id_type=MESH,
            )
            for d in range(1, shards)
        ]
        for copy in copies:
            copy.start()
        return copies

    def gathered(i):
        return [mom[i]] + [parts[i, d] for d in range(1, shards)]

    def pack(first, last):
        packed = rows_a[first]
        for b in range(first + 1, last):
            packed = packed + pltpu.roll(rows_a[b], 2 * segs * (b - first), 1)
        return packed

    def unpack(packed, dst, first, last):
        dst[first] = packed
        for b in range(first + 1, last):
            dst[b] = pltpu.roll(packed, LANES - 2 * segs * (b - first), 1)

    def column(d):
        return pl.ds(pl.multiple_of(peer_x[d] * width, LANES), width)

    def pieces(h):
        return [
            (own_dy.at[h], 0), (ring.at[h, 0], shards - 1), (ring.at[h, 1], 1), (ring.at[h, 2], 2)
        ]

    def stage(h, between, after):
        dy = own_dy.at[h]
        x_own = own_x.at[h]
        arrived(p_x.at[h], x_own, 4 + 2 * h)

        def moments(b, carry):
            x = x_own[pl.ds(b * (FB // 2), FB // 2)].astype(F32).reshape(FB, segs, width)
            mean = jnp.sum(x, axis=2, keepdims=True) * (1.0 / width)
            centre = x - mean
            square = jnp.sum(centre * centre, axis=2, keepdims=True)
            rows_a[b] = to_row(mean, square, segs)
            return carry

        lax.fori_loop(0, blocks, moments, 0)
        mom[3 * h] = pack(0, blocks)
        copies = exchange(3 * h)
        for copy in rings[h][:4]:
            copy.wait_recv()
        rings[h][4].start()
        rings[h][5].start()

        def hid_rows(b, chosen):
            acc = None
            for piece, d in chosen:
                rows = piece[pl.ds(b * FB, FB)].reshape(2 * FB * segs, width)
                term = lax.dot_general(
                    rows, w_vmem[:, column(d)], (((1,), (1,)), ((), ())), preferred_element_type=F32
                )
                acc = term if acc is None else acc + term
            return acc.reshape(2 * FB, segs, width)

        def hid_near(b, carry):
            hid[pl.ds(b * 2 * FB, 2 * FB)] = hid_rows(b, pieces(h)[:3])
            return carry

        def hid_far(b, carry):
            at = pl.ds(b * 2 * FB, 2 * FB)
            hid[at] = hid[at] + hid_rows(b, pieces(h)[3:])
            return carry

        lax.fori_loop(0, blocks // 2, hid_near, 0)
        for copy in copies:
            copy.wait()
        mean_row, scale_row = mean_and_scale(gathered(3 * h), width, segs)
        unpack(mean_row, rows_a, 0, blocks)
        unpack(scale_row, rows_b, 0, blocks)

        def normalize(b, carry):
            at = pl.ds(b * FB, FB)
            mean = to_column(rows_a[b], segs)
            scale = to_column(rows_b[b], segs)
            x = x_own[pl.ds(b * (FB // 2), FB // 2)].astype(F32).reshape(FB, segs, width)
            normed[at] = (x - mean) * scale
            scale_c[at] = jnp.broadcast_to(scale, (FB, segs, LANES))
            return carry

        lax.fori_loop(0, blocks, normalize, 0)

        def convolve(lb, carry):
            lanes = pl.ds(pl.multiple_of(lb * LANES, LANES), LANES)
            gain = gain_ref[:, lanes].astype(F32)

            def fill(i, c):
                at = pl.ds(i * FB, FB)
                spad[h, lb, pl.ds(i * FB + half, FB)] = normed[at, :, lanes] * gain[None]
                return c

            lax.fori_loop(0, blocks, fill, 0)

            def step(i, c):
                t = i * STEP
                acc = tapb[0, :, lanes][None] * spad[h, lb, pl.ds(t, STEP)]
                for k in range(1, taps):
                    acc = acc + tapb[k, :, lanes][None] * spad[h, lb, pl.ds(t + k, STEP)]
                gate = 1.0 / (1.0 + jnp.exp(-acc))
                out = acc * gate
                slope[pl.ds(t, STEP), :, lanes] = gate + out * (1.0 - gate)
                hidden[h, pl.ds(t, STEP), :, lanes] = out.astype(BF16)
                return c

            lax.fori_loop(0, frames // STEP, step, 0)
            return carry

        lax.fori_loop(0, chunks, convolve, 0)
        rings[h][4].wait_recv()
        rings[h][5].wait_recv()
        lax.fori_loop(0, blocks // 2, hid_far, 0)
        between()
        sum_a[...] = jnp.zeros_like(sum_a)
        sum_b[...] = jnp.zeros_like(sum_b)

        def slopes(lb, carry):
            lanes = pl.ds(pl.multiple_of(lb * LANES, LANES), LANES)

            def fill(i, c):
                at = pl.ds(i * STEP, STEP)
                gpad[h, lb, pl.ds(i * STEP + half, STEP)] = hid[at, :, lanes] * slope[at, :, lanes]
                return c

            return lax.fori_loop(0, frames // STEP, fill, carry)

        lax.fori_loop(0, chunks, slopes, 0)

        def backward(first, last, lb, carry):
            lanes = pl.ds(pl.multiple_of(lb * LANES, LANES), LANES)
            gain = gain_ref[:, lanes].astype(F32)

            def transposed(i, gain_sum):
                t = i * STEP
                at = pl.ds(t, STEP)
                acc = tapb[0, :, lanes][None] * gpad[h, lb, pl.ds(t + taps - 1, STEP)]
                for k in range(1, taps):
                    acc = acc + tapb[k, :, lanes][None] * gpad[h, lb, pl.ds(t + taps - 1 - k, STEP)]
                hid[at, :, lanes] = acc
                cross = acc * normed[at, :, lanes]
                sum_a[at] = sum_a[at] + acc * gain[None]
                sum_b[at] = sum_b[at] + cross * gain[None]
                return gain_sum + jnp.sum(cross, axis=0)

            zero = jnp.zeros((segs, LANES), F32)
            gacc[:, lanes] = gacc[:, lanes] + lax.fori_loop(first, last, transposed, zero)

            return carry

        def sum_rows(b, carry):
            at = pl.ds(b * FB, FB)
            first = jnp.sum(sum_a[at], axis=2, keepdims=True)
            second = jnp.sum(sum_b[at], axis=2, keepdims=True)
            rows_a[b] = to_row(first, second, segs)
            return carry

        def prepare(b, carry):
            at = pl.ds(b * FB, FB)
            scale = scale_c[at][:, :, 0:1]
            grads = dy[pl.ds(b * (FB // 2), FB // 2)].astype(F32).reshape(FB, segs, width)
            hid[at] = grads + scale * (hid[at] * gain_ref[...].astype(F32)[None])
            normed[at] = scale * normed[at]
            return carry

        def finish(b, carry):
            at = pl.ds(b * FB, FB)
            plain = to_column(rows_a[b], segs)
            cross = to_column(rows_b[b], segs)
            scale = scale_c[at][:, :, 0:1]
            out = (hid[at] - scale * plain - normed[at] * cross).astype(BF16)
            out = out.reshape(FB // 2, 2, segs, width)
            for j in range(2):
                ret[h, j, pl.ds(b * (FB // 2), FB // 2)] = out[:, j]
            return carry

        spans = [(0, blocks // 2), (blocks // 2, blocks)]
        steps = FB // STEP
        copies = []
        for c, (first, last) in enumerate(spans):
            lax.fori_loop(0, chunks, functools.partial(backward, first * steps, last * steps), 0)
            lax.fori_loop(first, last, sum_rows, 0)
            mom[3 * h + 1 + c] = pack(first, last)
            copies.append(exchange(3 * h + 1 + c))
        after()
        for c, (first, last) in enumerate(spans):
            lax.fori_loop(first, last, prepare, 0)
            for copy in copies[c]:
                copy.wait()
            row = sum(gathered(3 * h + 1 + c)) * (1.0 / (shards * width))
            unpack(row, rows_a, first, last)
            unpack(pltpu.roll(row, LANES - segs, 1), rows_b, first, last)
            lax.fori_loop(first, last, finish, 0)
            for j in range(2):
                scatter_half(ret.at[h, j], back.at[h, j], 7 + 2 * h + j, c)

    loads[2].wait()
    start_ring(0)
    go_on_ring(0)
    stage(0, lambda: start_ring(1), lambda: go_on_ring(1))
    stage(1, lambda: None, lambda: None)

    def tap_grads(lb, carry):
        lanes = pl.ds(pl.multiple_of(lb * LANES, LANES), LANES)
        for h in range(2):

            def tap_sums(i, c):
                t = i * STEP
                g = gpad[h, lb, pl.ds(t + half, STEP)]
                for k in range(taps):
                    term = jnp.sum(g * spad[h, lb, pl.ds(t + k, STEP)], axis=0)
                    kacc[k, :, lanes] = kacc[k, :, lanes] + term
                return c

            lax.fori_loop(0, frames // STEP, tap_sums, 0)
        return carry

    def weights():
        lax.fori_loop(0, chunks, tap_grads, 0)
        for k in range(taps):
            kgrad_ref[k] = jnp.sum(kacc[k], axis=0, keepdims=True)
        ggrad_ref[...] = jnp.sum(gacc[...], axis=0, keepdims=True)
        rows_of = frames * segs
        for j in range(shards):
            block = None
            for h in range(2):
                piece, d = pieces(h)[j]
                term = lax.dot_general(
                    hidden[h].reshape(rows_of, width), piece[...].reshape(rows_of, width),
                    (((0,), (0,)), ((), ())), preferred_element_type=F32,
                )
                block = term if block is None else block + term
            w_block[:, column(d)] = (block * grad_scale).astype(BF16)

    weights()
    w_store = pltpu.make_async_copy(w_block, wgrad_ref, load.at[3])
    w_store.start()
    sent(s0, r0, 1)
    for j in range(2):
        for h in range(2):
            arrived(ret.at[h, j], back.at[h, j], 7 + 2 * h + j)
        permute_home(j, home.at[j])
        scatter(home.at[j], home_ref.at[j], 11 + j, same, pair_of)
    sent(langs_own, langs_all, 0)
    sent(s1, r1, 2)
    for h in range(2):
        sent(p_dy.at[h], own_dy.at[h], 3 + 2 * h)
        sent(p_x.at[h], own_x.at[h], 4 + 2 * h)
        for j in range(2):
            sent(ret.at[h, j], back.at[h, j], 7 + 2 * h + j)
        for copy in rings[h]:
            copy.wait_send()
    w_store.wait()
    for j in range(2):
        arrived(home.at[j], home_ref.at[j], 11 + j)
        sent(home.at[j], home_ref.at[j], 11 + j)


def deliver_kernel(grad_scale, home_ref, w_ref, g_ref, k_ref, feat_ref, wgrad_ref, ggrad_ref, kgrad_ref):
    segs, frames, width = feat_ref.shape

    def join_frames(b, carry):
        at = pl.ds(b * (FB // 2), FB // 2)
        rows = jnp.stack([home_ref[0, at].astype(F32), home_ref[1, at].astype(F32)], axis=1)
        rows = rows.reshape(FB, segs, width)
        feat_ref[:, pl.ds(pl.multiple_of(b * FB, FB), FB), :] = jnp.swapaxes(rows, 0, 1).astype(BF16)
        return carry

    lax.fori_loop(0, frames // FB, join_frames, 0)
    wgrad_ref[...] = w_ref[...]
    ggrad_ref[...] = g_ref[...] * grad_scale
    kgrad_ref[...] = k_ref[...] * grad_scale


def per_device(feats, cotan, lang, w_out, gain, kernel):
    segs, frames, width = feats.shape
    owners = lax.axis_size("expert")
    shards = lax.axis_size("fsdp")
    taps = kernel.shape[1]
    total = owners * segs
    grad_scale = float(segs * frames) ** (-0.5)
    shape = jax.ShapeDtypeStruct
    half = segs // 2
    whole = pltpu.VMEM((owners, frames // owners, segs, width), BF16)
    halves = (owners, frames // owners, half, width)
    f32_rows = pltpu.VMEM((frames, half, width), F32)
    columns = pltpu.VMEM((frames, half, LANES), F32)
    padded = pltpu.VMEM((2, width // LANES, frames + 32, half, LANES), F32)
    rows = pltpu.VMEM((frames // FB, FB, LANES), F32)
    dma = pltpu.SemaphoreType.DMA
    vmem = pl.BlockSpec(memory_space=pltpu.VMEM)
    home, w_grad, gain_grad, tap_grad = pl.pallas_call(
        functools.partial(module_kernel, owners, shards, grad_scale),
        out_shape=(
            shape((2, owners, segs, width), BF16),
            shape(w_out.shape[1:], BF16),
            shape((1, width), F32),
            shape((taps, 1, width), F32),
        ),
        in_specs=[pl.BlockSpec(memory_space=pltpu.SMEM)] + [pl.BlockSpec(memory_space=pl.ANY)] * 3 + [vmem] * 2,
        out_specs=(pl.BlockSpec(memory_space=pl.ANY),) * 2 + (vmem,) * 2,
        scratch_shapes=[
            pltpu.VMEM(feats.shape, BF16),
            pltpu.VMEM(feats.shape, BF16),
            pltpu.VMEM(w_out.shape[1:], BF16),
            pltpu.VMEM((2, owners, 1, LANES), F32),
            *[whole] * 4,
            *[pltpu.VMEM((2,) + halves, BF16)] * 4,
            pltpu.VMEM((2, shards - 1) + halves, BF16),
            pltpu.VMEM((2, 2, owners, half, width), BF16),
            pltpu.VMEM((2, 2, owners, half, width), BF16),
            pltpu.VMEM((2, owners, segs, width), BF16),
            pltpu.VMEM((total, total), BF16),
            pltpu.VMEM((total, total), BF16),
            f32_rows,
            f32_rows,
            pltpu.VMEM((2, frames, half, width), BF16),
            f32_rows,
            padded,
            padded,
            pltpu.VMEM((taps, half, width), F32),
            pltpu.VMEM((taps, half, width), F32),
            pltpu.VMEM((half, width), F32),
            columns,
            columns,
            columns,
            rows,
            rows,
            pltpu.VMEM((6, FB, LANES), F32),
            pltpu.VMEM((6, shards, FB, LANES), F32),
            dma((13,)),
            dma((13,)),
            dma((2, 6)),
            dma((2, 6)),
            dma((6, shards)),
            dma((6, shards)),
            dma((4,)),
            pltpu.VMEM(w_out.shape[1:], BF16),
        ],
        compiler_params=pltpu.CompilerParams(
            collective_id=0, has_side_effects=True, vmem_limit_bytes=67043328
        ),
        name="module_backward",
    )(lang, feats, cotan, w_out[0], gain, kernel[0])
    feat_grad, w_grad, gain_grad, tap_grad = pl.pallas_call(
        functools.partial(deliver_kernel, grad_scale),
        out_shape=(
            shape((segs, frames, width), BF16),
            shape(w_out.shape[1:], BF16),
            shape((1, width), F32),
            shape((taps, 1, width), F32),
        ),
        in_specs=[vmem] * 4,
        out_specs=(vmem,) * 4,
        name="deliver",
    )(home, w_grad, gain_grad, tap_grad)
    return feat_grad, w_grad[None], gain_grad, jnp.swapaxes(tap_grad, 0, 1)


def solution(mesh):
    in_specs = (
        P("expert", None, "fsdp"),
        P("expert", None, "fsdp"),
        P("expert"),
        P("expert", "fsdp", None),
        P("expert", "fsdp"),
        P("expert", None, "fsdp"),
    )
    out_specs = (
        P("expert", None, "fsdp"),
        P("expert", "fsdp", None),
        P("expert", "fsdp"),
        P("expert", None, "fsdp"),
    )
    return jax.shard_map(
        per_device, mesh=mesh, in_specs=in_specs, out_specs=out_specs, check_vma=False
    )
```

```python
import functools

import jax
import jax.numpy as jnp
from jax import lax
from jax.experimental import pallas as pl
from jax.experimental.pallas import tpu as pltpu
from jax.sharding import PartitionSpec as P

MESH = pl.DeviceIdType.MESH
F32 = jnp.float32
BF16 = jnp.bfloat16
LANES = 128
STEP = 16
FB = 16


def diagonal(segs):
    lane = lax.broadcasted_iota(jnp.int32, (1, segs, LANES), 2)
    seg = lax.broadcasted_iota(jnp.int32, (1, segs, LANES), 1)
    return lane == seg, lane == seg + segs


def to_row(first, second, segs):
    low, high = diagonal(segs)
    spread = jnp.where(low, first, 0.0) + jnp.where(high, second, 0.0)
    return jnp.sum(spread, axis=1)


def to_column(row, segs):
    low, _ = diagonal(segs)
    return jnp.sum(jnp.where(low, row[:, None, :], 0.0), axis=2, keepdims=True)


def mean_and_scale(rows, width, segs):
    n = len(rows)
    squares = [pltpu.roll(r, LANES - segs, 1) for r in rows]
    mean = sum(rows) * (1.0 / n)
    spread = sum((r - mean) * (r - mean) for r in rows)
    var = (sum(squares) + width * spread) * (1.0 / (n * width))
    return mean, lax.rsqrt(var + 1e-05)


def module_kernel(
    owners, shards, grad_scale,
    lang_ref, x_ref, dy_ref, w_ref, gain_ref, taps_ref,
    home_ref, wgrad_ref, ggrad_ref, kgrad_ref,
    x_vmem, dy_vmem, w_vmem, langs, s0, s1, r0, r1, p_dy, p_x, own_dy, own_x, ring, ret, back, home, pick, pick_t,
    normed, slope, hidden, hid, gpad, spad, tapb, kacc, gacc, sum_a, sum_b, scale_c, rows_a, rows_b, mom, parts,
    send, recv, ring_send, ring_recv, ex_send, ex_recv, load, w_block,
):
    all_segs, frames, width = x_ref.shape
    segs = own_x.shape[3]
    taps = taps_ref.shape[0]
    half = taps // 2
    total = owners * all_segs
    part = owners * segs
    chunks = width // LANES
    blocks = frames // FB
    me = lax.axis_index("expert")
    fs = lax.axis_index("fsdp")
    peer_x = [lax.rem(fs + d, shards) for d in range(shards)]

    barrier = pltpu.get_barrier_semaphore()

    def greet(d, carry):
        pl.semaphore_signal(
            barrier, inc=1, device_id={"expert": lax.rem(me + d, owners)}, device_id_type=MESH
        )
        return carry

    loads = [
        pltpu.make_async_copy(src, dst, load.at[i])
        for i, (src, dst) in enumerate(((dy_ref, dy_vmem), (x_ref, x_vmem), (w_ref, w_vmem)))
    ]
    for copy in loads:
        copy.start()
    lax.fori_loop(1, owners, greet, 0)
    for d in range(1, shards):
        pl.semaphore_signal(barrier, inc=1, device_id={"fsdp": peer_x[d]}, device_id_type=MESH)

    def split_frames(src, dst):
        def block(b, carry):
            rows = src[:, pl.ds(pl.multiple_of(b * FB, FB), FB), :].astype(F32)
            moved = jnp.swapaxes(rows, 0, 1).astype(BF16)
            dst[pl.ds(b * (FB // 2), FB // 2)] = moved.reshape(FB // 2, 2, all_segs, width)
            return carry

        lax.fori_loop(0, blocks, block, 0)

    def pair_of(p):
        return lax.rem(p, 2) * (owners // 2) + lax.div(p, 2)

    def same(p):
        return p

    def send_block(src, dst, i, p, src_at, dst_at):
        pltpu.make_async_remote_copy(
            src_ref=src.at[src_at(p)], dst_ref=dst.at[dst_at(me)], send_sem=send.at[i], recv_sem=recv.at[i],
            device_id={"expert": p}, device_id_type=MESH,
        ).start()

    def keep_block(src, dst, i, src_at, dst_at):
        pltpu.make_async_copy(src.at[src_at(me)], dst.at[dst_at(me)], recv.at[i]).start()

    def scatter(src, dst, i, src_at, dst_at):
        def both(d, carry):
            send_block(src, dst, i, lax.rem(me + d, owners), src_at, dst_at)
            send_block(src, dst, i, lax.rem(me + owners - d, owners), src_at, dst_at)
            return carry

        lax.fori_loop(1, owners // 2, both, 0)
        send_block(src, dst, i, lax.rem(me + owners // 2, owners), src_at, dst_at)
        keep_block(src, dst, i, src_at, dst_at)

    def scatter_half(src, dst, i, c):
        count = owners // 2
        mine = lax.div(me, 2)

        def one(d, carry):
            send_block(src, dst, i, lax.rem(mine + d, count) * 2 + c, pair_of, same)
            return carry

        lax.fori_loop(1, count, one, 0)

        @pl.when(lax.rem(me, 2) == c)
        def _():
            keep_block(src, dst, i, pair_of, same)

        @pl.when(lax.rem(me, 2) != c)
        def _():
            send_block(src, dst, i, mine * 2 + c, pair_of, same)

    def arrived(src, dst, i):
        pltpu.make_async_copy(src, dst, recv.at[i]).wait()

    def sent(src, dst, i):
        most = pl.ds(0, owners - 1)
        pltpu.make_async_remote_copy(
            src_ref=src.at[most], dst_ref=dst.at[most], send_sem=send.at[i], recv_sem=recv.at[i],
            device_id={"expert": lax.rem(me + 1, owners)}, device_id_type=MESH,
        ).wait_send()

    lane = lax.broadcasted_iota(jnp.int32, (1, LANES), 1)
    first_lane = lax.rem(me, LANES // all_segs) * all_segs
    lang_row = jnp.zeros((1, LANES), jnp.int32)
    for i in range(all_segs):
        lang_row = jnp.where(lane == first_lane + i, lang_ref[i], lang_row)
    lang_row = lang_row.astype(F32)
    loads[0].wait()
    split_frames(dy_vmem, s0)
    langs_own = langs.at[0]
    langs_all = langs.at[1]

    def spread_langs(d, carry):
        langs_own[d] = lang_row
        return carry

    lax.fori_loop(0, owners, spread_langs, 0)
    pl.semaphore_wait(barrier, owners - 1 + shards - 1)
    scatter(langs_own, langs_all, 0, same, same)
    scatter(s0, r0, 1, pair_of, same)
    loads[1].wait()
    split_frames(x_vmem, s1)
    scatter(s1, r1, 2, pair_of, same)

    for k in range(taps):
        tapb[k] = jnp.broadcast_to(taps_ref[k : k + 1, :].astype(F32), (segs, width))
    for pad in (gpad, spad):
        for h in range(2):
            for c in range(chunks):
                pad[h, c, :half] = jnp.zeros((half, segs, LANES), F32)
                pad[h, c, half + frames :] = jnp.zeros((pad.shape[2] - half - frames, segs, LANES), F32)
    kacc[...] = jnp.zeros_like(kacc)
    gacc[...] = jnp.zeros_like(gacc)

    arrived(langs_own, langs_all, 0)
    owner_of = lax.broadcasted_iota(jnp.int32, (owners, LANES), 0).astype(F32)
    before = lax.broadcasted_iota(jnp.int32, (LANES, LANES), 0) < lax.broadcasted_iota(
        jnp.int32, (LANES, LANES), 1
    )
    before = jnp.where(before, 1.0, 0.0).astype(BF16)
    place = lax.broadcasted_iota(jnp.int32, (total, LANES), 0).astype(F32)
    base = jnp.zeros((owners, 1), F32)
    group = LANES // all_segs
    for q in range(total // LANES):
        row = jnp.sum(langs_all[q * group : (q + 1) * group], axis=0)
        match = jnp.where(owner_of == row, 1.0, 0.0)
        rank = jnp.dot(match.astype(BF16), before, preferred_element_type=F32) + base
        base = base + jnp.sum(match, axis=1, keepdims=True)
        spot = owner_of * segs + rank + jnp.where(rank >= segs, float(part - segs), 0.0)
        dest = jnp.sum(match * spot, axis=0, keepdims=True)
        pick[:, q * LANES : (q + 1) * LANES] = jnp.where(place == dest, 1.0, 0.0).astype(BF16)
    number = lax.broadcasted_iota(jnp.int32, (16, total), 1)
    which = lax.broadcasted_iota(jnp.int32, (16, total), 0)
    digits = jnp.where(which == 0, number // 32, number % 32).astype(F32).astype(BF16)
    found = lax.dot_general(digits, pick[...], (((1,), (1,)), ((), ())), preferred_element_type=F32)
    source = found[0:1] * 32.0 + found[1:2]
    for q in range(total // LANES):
        cols = slice(q * LANES, (q + 1) * LANES)
        pick_t[:, cols] = jnp.where(place == source[:, cols], 1.0, 0.0).astype(BF16)

    def permute_out(h, src, dst):
        rows = 256

        def block(b, carry):
            choice = pick[pl.ds(pl.multiple_of(h * part + b * rows, rows), rows), :]
            for j in range(2):
                flat = src[:, j].reshape(total, width)
                moved = jnp.dot(choice, flat, preferred_element_type=F32).astype(BF16)
                dst[pl.ds(b * (rows // segs), rows // segs), j] = moved.reshape(rows // segs, segs, width)
            return carry

        lax.fori_loop(0, part // rows, block, 0)

    def permute_home(j, dst):
        rows = 256

        def block(b, carry):
            at = pl.ds(pl.multiple_of(b * rows, rows), rows)
            moved = None
            for h in range(2):
                flat = back[h, j].reshape(part, width)
                term = jnp.dot(pick_t[at, h * part : (h + 1) * part], flat, preferred_element_type=F32)
                moved = term if moved is None else moved + term
            moved = moved.astype(BF16).reshape(rows // all_segs, all_segs, width)
            dst[pl.ds(b * (rows // all_segs), rows // all_segs)] = moved
            return carry

        lax.fori_loop(0, total // rows, block, 0)

    arrived(s0, r0, 1)
    permute_out(0, r0, p_dy.at[0])
    scatter(p_dy.at[0], own_dy.at[0], 3, same, pair_of)
    permute_out(1, r0, p_dy.at[1])
    arrived(s1, r1, 2)
    permute_out(0, r1, p_x.at[0])
    scatter(p_x.at[0], own_x.at[0], 4, same, pair_of)
    scatter(p_dy.at[1], own_dy.at[1], 5, same, pair_of)
    permute_out(1, r1, p_x.at[1])
    scatter(p_x.at[1], own_x.at[1], 6, same, pair_of)

    def ring_copy(h, src, dst, i, d):
        return pltpu.make_async_remote_copy(
            src_ref=src, dst_ref=dst, send_sem=ring_send.at[h, i], recv_sem=ring_recv.at[h, i],
            device_id={"fsdp": peer_x[d]}, device_id_type=MESH,
        )

    middle = owners // 2

    def ring_copies(h):
        own = own_dy.at[h]
        one = ring.at[h, 0]
        two = ring.at[h, 1]
        far = ring.at[h, 2]
        low = pl.ds(0, middle)
        high = pl.ds(middle, middle)
        return [
            ring_copy(h, own.at[low], one.at[low], 0, 1),
            ring_copy(h, own.at[high], two.at[high], 1, shards - 1),
            ring_copy(h, own.at[high], one.at[high], 2, 1),
            ring_copy(h, own.at[low], two.at[low], 3, shards - 1),
            ring_copy(h, one.at[low], far.at[low], 4, 1),
            ring_copy(h, two.at[high], far.at[high], 5, shards - 1),
        ]

    rings = [ring_copies(0), ring_copies(1)]

    def start_ring(h):
        arrived(p_dy.at[h], own_dy.at[h], 3 + 2 * h)
        rings[h][0].start()
        rings[h][1].start()

    def go_on_ring(h):
        rings[h][2].start()
        rings[h][3].start()

    def exchange(i):
        copies = [
            pltpu.make_async_remote_copy(
                src_ref=mom.at[i], dst_ref=parts.at[i, d], send_sem=ex_send.at[i, d],
                recv_sem=ex_recv.at[i, d], device_id={"fsdp": peer_x[d]}, device_id_type=MESH,
            )
            for d in range(1, shards)
        ]
        for copy in copies:
            copy.start()
        return copies

    def gathered(i):
        return [mom[i]] + [parts[i, d] for d in range(1, shards)]

    def pack(first, last):
        packed = rows_a[first]
        for b in range(first + 1, last):
            packed = packed + pltpu.roll(rows_a[b], 2 * segs * (b - first), 1)
        return packed

    def unpack(packed, dst, first, last):
        dst[first] = packed
        for b in range(first + 1, last):
            dst[b] = pltpu.roll(packed, LANES - 2 * segs * (b - first), 1)

    def column(d):
        return pl.ds(pl.multiple_of(peer_x[d] * width, LANES), width)

    def pieces(h):
        return [
            (own_dy.at[h], 0), (ring.at[h, 0], shards - 1), (ring.at[h, 1], 1), (ring.at[h, 2], 2)
        ]

    def stage(h, between, after):
        dy = own_dy.at[h]
        x_own = own_x.at[h]
        arrived(p_x.at[h], x_own, 4 + 2 * h)

        def moments(b, carry):
            x = x_own[pl.ds(b * (FB // 2), FB // 2)].astype(F32).reshape(FB, segs, width)
            mean = jnp.sum(x, axis=2, keepdims=True) * (1.0 / width)
            centre = x - mean
            square = jnp.sum(centre * centre, axis=2, keepdims=True)
            rows_a[b] = to_row(mean, square, segs)
            return carry

        lax.fori_loop(0, blocks, moments, 0)
        mom[3 * h] = pack(0, blocks)
        copies = exchange(3 * h)
        for copy in rings[h][:4]:
            copy.wait_recv()
        rings[h][4].start()
        rings[h][5].start()

        def hid_rows(b, chosen):
            acc = None
            for piece, d in chosen:
                rows = piece[pl.ds(b * FB, FB)].reshape(2 * FB * segs, width)
                term = lax.dot_general(
                    rows, w_vmem[:, column(d)], (((1,), (1,)), ((), ())), preferred_element_type=F32
                )
                acc = term if acc is None else acc + term
            return acc.reshape(2 * FB, segs, width)

        def hid_near(b, carry):
            hid[pl.ds(b * 2 * FB, 2 * FB)] = hid_rows(b, pieces(h)[:3])
            return carry

        def hid_far(b, carry):
            at = pl.ds(b * 2 * FB, 2 * FB)
            hid[at] = hid[at] + hid_rows(b, pieces(h)[3:])
            return carry

        lax.fori_loop(0, blocks // 2, hid_near, 0)
        for copy in copies:
            copy.wait()
        mean_row, scale_row = mean_and_scale(gathered(3 * h), width, segs)
        unpack(mean_row, rows_a, 0, blocks)
        unpack(scale_row, rows_b, 0, blocks)

        def normalize(b, carry):
            at = pl.ds(b * FB, FB)
            mean = to_column(rows_a[b], segs)
            scale = to_column(rows_b[b], segs)
            x = x_own[pl.ds(b * (FB // 2), FB // 2)].astype(F32).reshape(FB, segs, width)
            normed[at] = (x - mean) * scale
            scale_c[at] = jnp.broadcast_to(scale, (FB, segs, LANES))
            return carry

        lax.fori_loop(0, blocks, normalize, 0)

        def convolve(lb, carry):
            lanes = pl.ds(pl.multiple_of(lb * LANES, LANES), LANES)
            gain = gain_ref[:, lanes].astype(F32)

            def fill(i, c):
                at = pl.ds(i * FB, FB)
                spad[h, lb, pl.ds(i * FB + half, FB)] = normed[at, :, lanes] * gain[None]
                return c

            lax.fori_loop(0, blocks, fill, 0)

            def step(i, c):
                t = i * STEP
                acc = tapb[0, :, lanes][None] * spad[h, lb, pl.ds(t, STEP)]
                for k in range(1, taps):
                    acc = acc + tapb[k, :, lanes][None] * spad[h, lb, pl.ds(t + k, STEP)]
                gate = 1.0 / (1.0 + jnp.exp(-acc))
                out = acc * gate
                slope[pl.ds(t, STEP), :, lanes] = gate + out * (1.0 - gate)
                hidden[h, pl.ds(t, STEP), :, lanes] = out.astype(BF16)
                return c

            lax.fori_loop(0, frames // STEP, step, 0)
            return carry

        lax.fori_loop(0, chunks, convolve, 0)
        rings[h][4].wait_recv()
        rings[h][5].wait_recv()
        lax.fori_loop(0, blocks // 2, hid_far, 0)
        between()
        sum_a[...] = jnp.zeros_like(sum_a)
        sum_b[...] = jnp.zeros_like(sum_b)

        def slopes(lb, carry):
            lanes = pl.ds(pl.multiple_of(lb * LANES, LANES), LANES)

            def fill(i, c):
                at = pl.ds(i * STEP, STEP)
                gpad[h, lb, pl.ds(i * STEP + half, STEP)] = hid[at, :, lanes] * slope[at, :, lanes]
                return c

            return lax.fori_loop(0, frames // STEP, fill, carry)

        lax.fori_loop(0, chunks, slopes, 0)

        def backward(first, last, lb, carry):
            lanes = pl.ds(pl.multiple_of(lb * LANES, LANES), LANES)
            gain = gain_ref[:, lanes].astype(F32)

            def transposed(i, gain_sum):
                t = i * STEP
                at = pl.ds(t, STEP)
                acc = tapb[0, :, lanes][None] * gpad[h, lb, pl.ds(t + taps - 1, STEP)]
                for k in range(1, taps):
                    acc = acc + tapb[k, :, lanes][None] * gpad[h, lb, pl.ds(t + taps - 1 - k, STEP)]
                hid[at, :, lanes] = acc
                cross = acc * normed[at, :, lanes]
                sum_a[at] = sum_a[at] + acc * gain[None]
                sum_b[at] = sum_b[at] + cross * gain[None]
                return gain_sum + jnp.sum(cross, axis=0)

            zero = jnp.zeros((segs, LANES), F32)
            gacc[:, lanes] = gacc[:, lanes] + lax.fori_loop(first, last, transposed, zero)

            return carry

        def sum_rows(b, carry):
            at = pl.ds(b * FB, FB)
            first = jnp.sum(sum_a[at], axis=2, keepdims=True)
            second = jnp.sum(sum_b[at], axis=2, keepdims=True)
            rows_a[b] = to_row(first, second, segs)
            return carry

        def prepare(b, carry):
            at = pl.ds(b * FB, FB)
            scale = scale_c[at][:, :, 0:1]
            grads = dy[pl.ds(b * (FB // 2), FB // 2)].astype(F32).reshape(FB, segs, width)
            hid[at] = grads + scale * (hid[at] * gain_ref[...].astype(F32)[None])
            normed[at] = scale * normed[at]
            return carry

        def finish(b, carry):
            at = pl.ds(b * FB, FB)
            plain = to_column(rows_a[b], segs)
            cross = to_column(rows_b[b], segs)
            scale = scale_c[at][:, :, 0:1]
            out = (hid[at] - scale * plain - normed[at] * cross).astype(BF16)
            out = out.reshape(FB // 2, 2, segs, width)
            for j in range(2):
                ret[h, j, pl.ds(b * (FB // 2), FB // 2)] = out[:, j]
            return carry

        spans = [(0, blocks // 2), (blocks // 2, blocks)]
        steps = FB // STEP
        copies = []
        for c, (first, last) in enumerate(spans):
            lax.fori_loop(0, chunks, functools.partial(backward, first * steps, last * steps), 0)
            lax.fori_loop(first, last, sum_rows, 0)
            mom[3 * h + 1 + c] = pack(first, last)
            copies.append(exchange(3 * h + 1 + c))
        after()
        for c, (first, last) in enumerate(spans):
            lax.fori_loop(first, last, prepare, 0)
            for copy in copies[c]:
                copy.wait()
            row = sum(gathered(3 * h + 1 + c)) * (1.0 / (shards * width))
            unpack(row, rows_a, first, last)
            unpack(pltpu.roll(row, LANES - segs, 1), rows_b, first, last)
            lax.fori_loop(first, last, finish, 0)
            for j in range(2):
                scatter_half(ret.at[h, j], back.at[h, j], 7 + 2 * h + j, c)

    loads[2].wait()
    start_ring(0)
    go_on_ring(0)
    stage(0, lambda: start_ring(1), lambda: go_on_ring(1))
    stage(1, lambda: None, lambda: None)

    def tap_grads(lb, carry):
        lanes = pl.ds(pl.multiple_of(lb * LANES, LANES), LANES)
        for h in range(2):

            def tap_sums(i, c):
                t = i * STEP
                g = gpad[h, lb, pl.ds(t + half, STEP)]
                for k in range(taps):
                    term = jnp.sum(g * spad[h, lb, pl.ds(t + k, STEP)], axis=0)
                    kacc[k, :, lanes] = kacc[k, :, lanes] + term
                return c

            lax.fori_loop(0, frames // STEP, tap_sums, 0)
        return carry

    def weights():
        lax.fori_loop(0, chunks, tap_grads, 0)
        for k in range(taps):
            kgrad_ref[k] = jnp.sum(kacc[k], axis=0, keepdims=True)
        ggrad_ref[...] = jnp.sum(gacc[...], axis=0, keepdims=True)
        rows_of = frames * segs
        for j in range(shards):
            block = None
            for h in range(2):
                piece, d = pieces(h)[j]
                term = lax.dot_general(
                    hidden[h].reshape(rows_of, width), piece[...].reshape(rows_of, width),
                    (((0,), (0,)), ((), ())), preferred_element_type=F32,
                )
                block = term if block is None else block + term
            w_block[:, column(d)] = (block * grad_scale).astype(BF16)

    weights()
    w_store = pltpu.make_async_copy(w_block, wgrad_ref, load.at[3])
    w_store.start()
    sent(s0, r0, 1)
    for j in range(2):
        for h in range(2):
            arrived(ret.at[h, j], back.at[h, j], 7 + 2 * h + j)
        permute_home(j, home.at[j])
        scatter(home.at[j], home_ref.at[j], 11 + j, same, pair_of)
    sent(langs_own, langs_all, 0)
    sent(s1, r1, 2)
    for h in range(2):
        sent(p_dy.at[h], own_dy.at[h], 3 + 2 * h)
        sent(p_x.at[h], own_x.at[h], 4 + 2 * h)
        for j in range(2):
            sent(ret.at[h, j], back.at[h, j], 7 + 2 * h + j)
        for copy in rings[h]:
            copy.wait_send()
    w_store.wait()
    for j in range(2):
        arrived(home.at[j], home_ref.at[j], 11 + j)
        sent(home.at[j], home_ref.at[j], 11 + j)


def deliver_kernel(
    grad_scale, home_ref, w_ref, g_ref, k_ref, feat_ref, wgrad_ref, ggrad_ref, kgrad_ref,
    home, feat, w_block, load, store,
):
    segs, frames, width = feat.shape
    parts = 4
    pairs = frames // 2 // parts
    loads = [
        pltpu.make_async_copy(
            home_ref.at[:, p * pairs : (p + 1) * pairs], home.at[:, p * pairs : (p + 1) * pairs], load.at[p]
        )
        for p in range(parts)
    ]
    loads.append(pltpu.make_async_copy(w_ref, w_block, load.at[parts]))
    stores = [
        pltpu.make_async_copy(
            feat.at[:, 2 * p * pairs : 2 * (p + 1) * pairs],
            feat_ref.at[:, 2 * p * pairs : 2 * (p + 1) * pairs],
            store.at[p],
        )
        for p in range(parts)
    ]
    stores.append(pltpu.make_async_copy(w_block, wgrad_ref, store.at[parts]))
    for copy in loads:
        copy.start()

    def join_frames(b, carry):
        at = pl.ds(b * (FB // 2), FB // 2)
        rows = jnp.stack([home[0, at].astype(F32), home[1, at].astype(F32)], axis=1)
        rows = rows.reshape(FB, segs, width)
        feat[:, pl.ds(pl.multiple_of(b * FB, FB), FB), :] = jnp.swapaxes(rows, 0, 1).astype(BF16)
        return carry

    each = 2 * pairs // FB
    for p in range(parts):
        loads[p].wait()
        lax.fori_loop(p * each, (p + 1) * each, join_frames, 0)
        if p > 0:
            stores[p - 1].start()
    loads[parts].wait()
    stores[parts].start()
    ggrad_ref[...] = g_ref[...] * grad_scale
    kgrad_ref[...] = k_ref[...] * grad_scale
    stores[parts - 1].start()
    for copy in stores:
        copy.wait()


def per_device(feats, cotan, lang, w_out, gain, kernel):
    segs, frames, width = feats.shape
    owners = lax.axis_size("expert")
    shards = lax.axis_size("fsdp")
    taps = kernel.shape[1]
    total = owners * segs
    grad_scale = float(segs * frames) ** (-0.5)
    shape = jax.ShapeDtypeStruct
    half = segs // 2
    whole = pltpu.VMEM((owners, frames // owners, segs, width), BF16)
    halves = (owners, frames // owners, half, width)
    f32_rows = pltpu.VMEM((frames, half, width), F32)
    columns = pltpu.VMEM((frames, half, LANES), F32)
    padded = pltpu.VMEM((2, width // LANES, frames + 32, half, LANES), F32)
    rows = pltpu.VMEM((frames // FB, FB, LANES), F32)
    dma = pltpu.SemaphoreType.DMA
    vmem = pl.BlockSpec(memory_space=pltpu.VMEM)
    home, w_grad, gain_grad, tap_grad = pl.pallas_call(
        functools.partial(module_kernel, owners, shards, grad_scale),
        out_shape=(
            shape((2, owners, segs, width), BF16),
            shape(w_out.shape[1:], BF16),
            shape((1, width), F32),
            shape((taps, 1, width), F32),
        ),
        in_specs=[pl.BlockSpec(memory_space=pltpu.SMEM)] + [pl.BlockSpec(memory_space=pl.ANY)] * 3 + [vmem] * 2,
        out_specs=(pl.BlockSpec(memory_space=pl.ANY),) * 2 + (vmem,) * 2,
        scratch_shapes=[
            pltpu.VMEM(feats.shape, BF16),
            pltpu.VMEM(feats.shape, BF16),
            pltpu.VMEM(w_out.shape[1:], BF16),
            pltpu.VMEM((2, owners, 1, LANES), F32),
            *[whole] * 4,
            *[pltpu.VMEM((2,) + halves, BF16)] * 4,
            pltpu.VMEM((2, shards - 1) + halves, BF16),
            pltpu.VMEM((2, 2, owners, half, width), BF16),
            pltpu.VMEM((2, 2, owners, half, width), BF16),
            pltpu.VMEM((2, owners, segs, width), BF16),
            pltpu.VMEM((total, total), BF16),
            pltpu.VMEM((total, total), BF16),
            f32_rows,
            f32_rows,
            pltpu.VMEM((2, frames, half, width), BF16),
            f32_rows,
            padded,
            padded,
            pltpu.VMEM((taps, half, width), F32),
            pltpu.VMEM((taps, half, width), F32),
            pltpu.VMEM((half, width), F32),
            columns,
            columns,
            columns,
            rows,
            rows,
            pltpu.VMEM((6, FB, LANES), F32),
            pltpu.VMEM((6, shards, FB, LANES), F32),
            dma((13,)),
            dma((13,)),
            dma((2, 6)),
            dma((2, 6)),
            dma((6, shards)),
            dma((6, shards)),
            dma((4,)),
            pltpu.VMEM(w_out.shape[1:], BF16),
        ],
        compiler_params=pltpu.CompilerParams(
            collective_id=0, has_side_effects=True, vmem_limit_bytes=67043328
        ),
        name="module_backward",
    )(lang, feats, cotan, w_out[0], gain, kernel[0])
    feat_grad, w_grad, gain_grad, tap_grad = pl.pallas_call(
        functools.partial(deliver_kernel, grad_scale),
        out_shape=(
            shape((segs, frames, width), BF16),
            shape(w_out.shape[1:], BF16),
            shape((1, width), F32),
            shape((taps, 1, width), F32),
        ),
        in_specs=[pl.BlockSpec(memory_space=pl.ANY)] * 2 + [vmem] * 2,
        out_specs=(pl.BlockSpec(memory_space=pl.ANY),) * 2 + (vmem,) * 2,
        scratch_shapes=[
            pltpu.VMEM((2, owners, segs, width), BF16),
            pltpu.VMEM((segs, frames, width), BF16),
            pltpu.VMEM(w_out.shape[1:], BF16),
            dma((5,)),
            dma((5,)),
        ],
        name="deliver",
    )(home, w_grad, gain_grad, tap_grad)
    return feat_grad, w_grad[None], gain_grad, jnp.swapaxes(tap_grad, 0, 1)


def solution(mesh):
    in_specs = (
        P("expert", None, "fsdp"),
        P("expert", None, "fsdp"),
        P("expert"),
        P("expert", "fsdp", None),
        P("expert", "fsdp"),
        P("expert", None, "fsdp"),
    )
    out_specs = (
        P("expert", None, "fsdp"),
        P("expert", "fsdp", None),
        P("expert", "fsdp"),
        P("expert", None, "fsdp"),
    )
    return jax.shard_map(
        per_device, mesh=mesh, in_specs=in_specs, out_specs=out_specs, check_vma=False
    )
```
